256 devices in a mesh: group: 8 (over x, core), prompt: 32 (over z, y).
Axes of the slice: x: 4, y: 4, z: 8, core: 2. Of those that a mesh axis runs over, the one named last changes fastest.
Arguments:
- queries: bfloat16 [32, 8, 64, 3072], P('prompt', 'group'), may hold values from -48 to 48
- fresh_latent: bfloat16 [32, 8, 64, 576], P('prompt', 'group'), may hold values from -6 to 6
- latent_cache: bfloat16 [32, 8, 512, 576], P('prompt', 'group'), may hold values from -48 to 48
- selected: int32 [32, 8, 64], P('prompt', 'group'), may hold values from 0 to 511, as said below
- position: int32 [32, 8], P('prompt'), may hold values from 0 to 7, each once within a row
- latent_gain: bfloat16 [512], replicated, may hold values from 0.099609375 to 1.8984375
- kv_up: bfloat16 [512, 4096], P('prompt'), may hold values from -0.25 to 0.25
- out_weight: bfloat16 [2048, 2048], P('prompt'), may hold values from -0.125 to 0.125
Outputs:
- attended: bfloat16 [32, 8, 64, 2048], P('prompt', 'group')
- blended: bfloat16 [32, 8, 512, 576], P('prompt', 'group')
The draws below stay inside these ranges and needn't reach their ends.
Inputs may be any that keep to these rules, and one draw needn't show every extreme that they name: `selected`: the 64 indices of a group are distinct and increasing.
All inputs are finite; a program needn't handle non-finite values.
Results may differ from the reference program's by a relative error of at most 0.011.
Values may be sent and summed in bfloat16 or wider, within the bound.
A program may use at most 128 MiB of HBM per device.

```python
import jax
import jax.numpy as jnp
from jax import lax

D = 2048
H = 16
DN = 128
DR = 64
DV = 128
LAT = 512
GROUP_LEN = 512
SEL = 64
GROUPS = 8
PROMPTS = 32


def draw_queries(key, part):
    base = jnp.clip(jax.random.normal(key, (PROMPTS, GROUPS, SEL, H, DN + DR), jnp.float32), -6.0, 6.0)
    return base.reshape(PROMPTS, GROUPS, SEL, H * (DN + DR)).astype(jnp.bfloat16)


def draw_latent_cache(key, part):
    base = jnp.clip(jax.random.normal(key, (PROMPTS, GROUPS, GROUP_LEN, LAT + DR), jnp.float32), -6.0, 6.0)
    return base.astype(jnp.bfloat16)


def draw_selected(key, part):
    raw = jax.random.randint(key, (PROMPTS, GROUPS, GROUP_LEN), 0, 1048576)
    scores = raw * GROUP_LEN + jnp.arange(GROUP_LEN, dtype=jnp.int32)
    picked = jax.lax.top_k(scores, SEL)[1]
    return jnp.sort(picked, -1).astype(jnp.int32)


def level_of(stream_key, shape, split, low, largest):
    def one(axis_at, parts):
        steps = jax.random.uniform(jax.random.fold_in(jax.random.fold_in(stream_key, 6), axis_at), (parts,), jnp.float32, low / len(split), largest / len(split))
        return jnp.repeat(jnp.exp(steps), shape[axis_at] // parts).reshape((-1,) + (1,) * (len(shape) - axis_at - 1))

    level = one(*split[0])
    for cut in split[1:]:
        level = level * one(*cut)
    return level


def scatter_about(rng, extent, width, reach, split=(), held_as=jnp.bfloat16):
    entries = jax.random.normal(rng, extent, jnp.float32) * width
    if len(split) > 0:
        entries = level_of(rng, extent, split, -0.22, 0.18) * entries
    return jnp.clip(entries, min=-reach, max=reach).astype(held_as)


def setup_inputs(seed: int = 0) -> dict:
    seeds = jax.random.split(jax.random.key(seed), 9)
    return {
        "queries": draw_queries(jax.random.fold_in(seeds[8], 71), 0),
        "fresh_latent": scatter_about(seeds[1], (PROMPTS, GROUPS, SEL, LAT + DR), 1.0, 6.0, ((0, 32), (1, 8))),
        "latent_cache": draw_latent_cache(jax.random.fold_in(seeds[8], 71), 0),
        "selected": draw_selected(jax.random.fold_in(seeds[8], 71), 0),
        "position": jax.vmap(lambda own: jax.random.permutation(own, GROUPS))(jax.random.split(seeds[4], PROMPTS)).reshape((PROMPTS, GROUPS)).astype(jnp.int32),
        "latent_gain": jnp.clip(1.0 + 0.18 * jax.random.normal(seeds[5], (LAT,), jnp.float32), 0.099609375, 1.8984375).astype(jnp.bfloat16),
        "kv_up": scatter_about(seeds[6], (LAT, H * (DN + DV)), LAT ** -0.5, 0.25, ((0, 32),)),
        "out_weight": scatter_about(seeds[7], (H * DV, D), (H * DV) ** -0.5, 0.125, ((0, 32),)),
    }


def rope_rotate(values, places):
    half = values.shape[-1] // 2
    freqs = 10000.0 ** (-jnp.arange(half, dtype=jnp.float32) / half)
    angles = places[..., None] * freqs
    cosine = jnp.cos(angles)
    sine = jnp.sin(angles)
    first = values[..., :half]
    second = values[..., half:]
    return jnp.concatenate([first * cosine - second * sine, second * cosine + first * sine], -1)

def prepare_rows(fresh, gain, places):
    latent = fresh[..., :LAT].astype(jnp.float32)
    factor = lax.rsqrt(lax.optimization_barrier(jnp.mean(latent * latent, -1, keepdims=True)) + 1e-06)
    normed = latent * factor * gain.astype(jnp.float32)
    turned = rope_rotate(fresh[..., LAT:].astype(jnp.float32), places)
    return jnp.concatenate([normed, turned], -1).astype(jnp.bfloat16)

def reference(queries, fresh_latent, latent_cache, selected, position, latent_gain, kv_up, out_weight):
    place_int = (position[:, :, None] * GROUP_LEN + selected).astype(jnp.int32)
    places = place_int.astype(jnp.float32)
    fresh_rows = prepare_rows(fresh_latent, latent_gain, places)
    prompt_ids = jnp.arange(PROMPTS, dtype=jnp.int32)[:, None, None]
    group_ids = jnp.arange(GROUPS, dtype=jnp.int32)[None, :, None]
    blended = latent_cache.at[prompt_ids, group_ids, selected].set(fresh_rows)
    weights_kv = kv_up.reshape(LAT, H, DN + DV).astype(jnp.float32)
    shaped = queries.reshape(PROMPTS, GROUPS, SEL, H, DN + DR)
    absorbed = jnp.einsum('pcshd,lhd->pcshl', shaped[..., :DN].astype(jnp.float32), weights_kv[..., :DN], precision=lax.Precision.HIGHEST).astype(jnp.bfloat16)
    turned = rope_rotate(shaped[..., DN:].astype(jnp.float32), places[..., None]).astype(jnp.bfloat16)
    query_vec = jnp.concatenate([absorbed, turned], -1).reshape(PROMPTS, GROUPS * SEL, H, LAT + DR)
    key_place = (position[:, :, None] * GROUP_LEN + jnp.arange(GROUP_LEN, dtype=jnp.int32)[None, None, :]).astype(jnp.int32)
    key_place = key_place.reshape(PROMPTS, GROUPS * GROUP_LEN)
    scale = (DN + DR) ** (-0.5)

    def one_prompt(items):
        qvec, keys, qplace, kplace = items
        scores = jnp.einsum('qhe,ke->qhk', qvec.astype(jnp.float32), keys.astype(jnp.float32), precision=lax.Precision.HIGHEST) * scale
        mask = (kplace[None, :] <= qplace[:, None])[:, None, :]
        peak = lax.optimization_barrier(jnp.max(jnp.where(mask, scores, -1e+30), -1, keepdims=True))
        probs = jnp.where(mask, jnp.exp(scores - peak), 0.0)
        total = lax.optimization_barrier(jnp.sum(probs, -1))
        rounded = lax.optimization_barrier(probs.astype(jnp.bfloat16))
        mixed = jnp.einsum('qhk,kl->qhl', rounded.astype(jnp.float32), keys[:, :LAT].astype(jnp.float32), precision=lax.Precision.HIGHEST)
        return (mixed / total[..., None]).astype(jnp.bfloat16)
    latent_mix = lax.map(one_prompt, (query_vec, blended.reshape(PROMPTS, GROUPS * GROUP_LEN, LAT + DR), place_int.reshape(PROMPTS, GROUPS * SEL), key_place))
    heads = jnp.einsum('pqhl,lhv->pqhv', latent_mix.astype(jnp.float32), weights_kv[..., DN:], precision=lax.Precision.HIGHEST).astype(jnp.bfloat16)
    heads = heads.reshape(PROMPTS * GROUPS * SEL, H * DV)
    attended = jnp.dot(heads, out_weight, preferred_element_type=jnp.float32).astype(jnp.bfloat16)
    return (attended.reshape(PROMPTS, GROUPS, SEL, D), blended)
```

```python
import functools

import jax
import jax.numpy as jnp
import numpy as np
from jax import lax
from jax.experimental import pallas as pl
from jax.experimental.pallas import tpu as pltpu
from jax.sharding import PartitionSpec as P

D = 2048
H = 16
DN = 128
DR = 64
DV = 128
LAT = 512
KEY = LAT + DR
GROUP = 512
SEL = 64
BF = jnp.bfloat16
F32 = jnp.float32
MESH = pl.DeviceIdType.MESH
EXP_SCALE = float((DN + DR) ** (-0.5) * np.log2(np.e))
COPIES = 96
STAGES = (((0, 0), (0, 1)), ((-1, 0), (1, 1)), ((-1, 1), (1, 0)), ((2, 0), (2, 1)))


def nt(a, b):
    return lax.dot_general(a, b, (((1,), (1,)), ((), ())), preferred_element_type=F32)


def kernel(
    q_ref, fresh_ref, cache_ref, sel_ref, pos_ref, gain_ref, kv_ref, ow_ref, freq_ref,
    att_out, bl_out,
    kbuf, qmsg, qrecv, selmsg, selrecv, kk, kvv, wbuf, qa, qr, qpl, m_s, l_s, acc, hall, omsg, att,
    ssem, rsem, lsem,
):
    g = lax.axis_index("group")
    p = lax.axis_index("prompt")
    x, c = lax.div(g, 2), lax.rem(g, 2)
    z, y = lax.div(p, 4), lax.rem(p, 4)
    other = 1 - c
    used = [0]

    def remote(src, dst, to):
        n = used[0]
        used[0] += 1
        return pltpu.make_async_remote_copy(
            src_ref=src,
            dst_ref=dst,
            send_sem=ssem.at[n],
            recv_sem=rsem.at[n],
            device_id=to,
            device_id_type=MESH,
        )

    def in_group(d):
        return {"group": lax.rem(g + d, 8)}

    def chip(dx):
        return lax.rem(x + dx + 4, 4)

    def peer(dx):
        return {"group": chip(dx) * 2 + c}

    sibling = {"group": x * 2 + other}

    def along_z(d):
        return {"prompt": lax.rem(z + d, 8) * 4 + y}

    def along_y(d):
        return {"prompt": z * 4 + lax.rem(y + d, 4)}

    barrier = pltpu.get_barrier_semaphore()
    everyone = [in_group(d) for d in range(1, 8)]
    everyone += [along_z(d) for d in range(1, 8)] + [along_y(d) for d in range(1, 4)]
    for to in everyone:
        pl.semaphore_signal(barrier, inc=1, device_id=to, device_id_type=MESH)

    part = kv_ref[:, pl.ds(pl.multiple_of(g * 512, 512), 512)]
    kk[z, y] = jnp.concatenate([part[:, :128], part[:, 256:384]], axis=1)
    kvv[z, y] = jnp.concatenate([part[:, 128:256], part[:, 384:]], axis=1)
    wbuf[z, y] = ow_ref[:, pl.ds(pl.multiple_of(g * 256, 256), 256)]

    sel_row = sel_ref[...].astype(F32)
    eye = lax.broadcasted_iota(jnp.int32, (SEL, 128), 0) == lax.broadcasted_iota(
        jnp.int32, (SEL, 128), 1
    )
    selmsg[...] = sel_row
    sel_col = jnp.sum(jnp.where(eye, sel_row, 0.0), -1, keepdims=True)
    place = sel_col + (pos_ref[0, g] * GROUP).astype(F32)
    angles = place * freq_ref[...]
    cosine = jnp.cos(angles)
    lane = lax.broadcasted_iota(jnp.int32, (SEL, 128), 1)
    first = lax.rem(lane, 64) < 32
    low = lane < 64
    sine = jnp.sin(angles)
    sine = jnp.where(first, -sine, sine)

    def rotate(v):
        partner = jnp.where(first, pltpu.roll(v, 96, 1), pltpu.roll(v, 32, 1))
        return v * cosine + partner * sine

    for j in range(8):
        t0 = q_ref[:, j * 384 : j * 384 + 128]
        t1 = q_ref[:, j * 384 + 128 : j * 384 + 256].astype(F32)
        t2 = q_ref[:, j * 384 + 256 : j * 384 + 384].astype(F32)
        qmsg[j, :, :128] = t0
        second = jnp.where(low, pltpu.roll(t1, 64, 1), pltpu.roll(t2, 64, 1))
        qmsg[j, :, 128:256] = second.astype(BF)
        qmsg[j, :, 256:] = rotate(jnp.where(low, t1, t2)).astype(BF)

    pl.semaphore_wait(barrier, len(everyone))

    def gather_z(buf):
        return [remote(buf.at[z, y], buf.at[z, y], along_z(d)) for d in range(1, 8)]

    def gather_y(buf):
        return [remote(buf.at[:, y], buf.at[:, y], along_y(d)) for d in range(1, 4)]

    def start(copies):
        for copy in copies:
            copy.start()

    def received(copies):
        for copy in copies:
            copy.wait_recv()

    kk_z = gather_z(kk)
    start(kk_z)
    sends = list(kk_z)
    order = (4, 3, 5, 2, 6, 1, 7)
    sel_copies = [remote(selmsg, selrecv.at[g], in_group(d)) for d in order]
    start(sel_copies)
    q_copies = [remote(qmsg.at[lax.rem(g + d, 8)], qrecv.at[g], in_group(d)) for d in order]
    start(q_copies)
    sends += sel_copies + q_copies
    qrecv[g] = qmsg[g]
    selrecv[g] = selmsg[...]

    latent = fresh_ref[:, :LAT].astype(F32)
    factor = lax.rsqrt(jnp.mean(latent * latent, -1, keepdims=True) + 1e-06)
    normed = (latent * factor * gain_ref[...].astype(F32)).astype(BF)
    tail = fresh_ref[:, LAT:].astype(F32)
    turned = rotate(jnp.concatenate([tail, tail], axis=1)).astype(BF)
    columns = lax.broadcasted_iota(jnp.int32, (SEL, GROUP), 1).astype(F32)
    hit = (columns == sel_col).astype(F32)
    taken = jnp.max(hit, 0, keepdims=True) > 0.5
    hit = hit.astype(BF)

    def tn(a, b):
        return lax.dot_general(a, b, (((0,), (0,)), ((), ())), preferred_element_type=F32)

    top = jnp.where(taken, tn(normed, hit), cache_ref[:LAT, :].astype(F32)).astype(BF)
    bottom = jnp.where(taken, tn(turned, hit)[:DR], cache_ref[LAT:, :].astype(F32)).astype(BF)
    for half in range(2):
        cols = slice(half * 256, half * 256 + 256)
        kbuf[0, half, c, :LAT, :] = top[:, cols]
        kbuf[0, half, c, LAT:, :] = bottom[:, cols]

    own = [kbuf.at[0, half, c] for half in range(2)]
    to_sib = [remote(own[i], kbuf.at[0, i, c], sibling) for i in range(2)]
    right = [remote(own[0], kbuf.at[1, 0, c], peer(1)), remote(own[1], kbuf.at[2, 0, c], peer(1))]
    left = [remote(own[1], kbuf.at[1, 1, c], peer(-1)), remote(own[0], kbuf.at[2, 1, c], peer(-1))]
    start([right[0], left[0], to_sib[0], to_sib[1], right[1], left[1]])
    sends += to_sib + right + left
    to_hbm = [
        pltpu.make_async_copy(own[i], bl_out.at[:, pl.ds(i * 256, 256)], lsem.at[i])
        for i in range(2)
    ]
    start(to_hbm)

    kvv_z = gather_z(kvv)
    start(kvv_z)
    w_z = gather_z(wbuf)
    start(w_z)
    sends += kvv_z + w_z

    m_s[...] = jnp.full(m_s.shape, -1e30, F32)
    l_s[...] = jnp.zeros(l_s.shape, F32)
    acc[...] = jnp.zeros(acc.shape, F32)

    received(kk_z)
    kk_y = gather_y(kk)
    start(kk_y)
    sends += kk_y
    received(sel_copies)
    for src in range(8):
        column = jnp.sum(jnp.where(eye, selrecv[src], 0.0), -1, keepdims=True)
        column = column + (pos_ref[0, src] * GROUP).astype(F32)
        qpl[src * SEL : src * SEL + SEL, :] = column
        qpl[512 + src * SEL : 512 + src * SEL + SEL, :] = column
    received(q_copies)
    for src in range(8):
        pair = qrecv[src, :, 256:].astype(F32)
        qr[src * SEL : src * SEL + SEL, :] = pair[:, :DR].astype(BF)
        qr[512 + src * SEL : 512 + src * SEL + SEL, :] = pltpu.roll(pair, 64, 1)[:, :DR].astype(BF)
    received(kk_y)
    for head in range(2):
        lanes = slice(head * 128, head * 128 + 128)
        keys = kk[:, :, :, lanes].reshape(LAT, DN)
        plain = qrecv[:, :, lanes].reshape(512, DN)
        qa[head * 512 : head * 512 + 512, :] = nt(plain, keys).astype(BF)

    def attend(stage, core, head, last):
        rows = pl.ds(head * 512, 512) if isinstance(head, int) else pl.ds(pl.multiple_of(head * 512, 512), 512)
        place = qpl[rows, :]
        number = lax.broadcasted_iota(jnp.int32, (512, 256), 1).astype(F32)
        query, turned = qa[rows, :], qr[rows, :]
        scores = []
        for i, (dx, half) in enumerate(STAGES[stage]):
            base = pos_ref[0, chip(dx) * 2 + core] * GROUP + half * 256
            s = jnp.dot(query, kbuf[stage, i, core, :LAT, :], preferred_element_type=F32)
            s += jnp.dot(turned, kbuf[stage, i, core, LAT:, :], preferred_element_type=F32)
            scores.append(jnp.where(number <= place - base.astype(F32), s, -1e30))
        peak = jnp.maximum(jnp.max(scores[0], -1, keepdims=True), jnp.max(scores[1], -1, keepdims=True))
        old = m_s[rows, :]
        peak = jnp.maximum(old, peak)
        probs = [jnp.exp2((s - peak) * EXP_SCALE) for s in scores]
        decay = jnp.exp2((old - peak) * EXP_SCALE)
        total = l_s[rows, :] * decay + jnp.sum(probs[0] + probs[1], -1, keepdims=True)
        mixed = acc[rows, :] * decay
        for i in range(2):
            mixed += nt(probs[i].astype(BF), kbuf[stage, i, core, :LAT, :])
        if last:
            return (mixed / total).astype(BF)
        m_s[rows, :] = peak
        l_s[rows, :] = total
        acc[rows, :] = mixed

    def both_heads(stage, core):
        def body(head, carry):
            attend(stage, core, head, False)
            return carry

        lax.fori_loop(0, 2, body, 0)

    both_heads(0, c)
    received(to_sib)
    both_heads(0, other)
    received(kvv_z)
    kvv_y = gather_y(kvv)
    start(kvv_y)
    sends += kvv_y

    received([right[0], left[0]])
    relay = [
        remote(kbuf.at[1, 0, c], kbuf.at[3, 0, c], peer(1)),
        remote(kbuf.at[1, 1, c], kbuf.at[3, 1, c], peer(-1)),
    ]
    start(relay)
    sends += relay
    for stage in range(1, 4):
        if stage == 2:
            received([right[1], left[1]])
        if stage == 3:
            received(relay)
        forward = [remote(kbuf.at[stage, i, c], kbuf.at[stage, i, c], sibling) for i in range(2)]
        start(forward)
        sends += forward
        both_heads(stage, c)
        if stage == 1:
            received(w_z)
            w_y = gather_y(wbuf)
            start(w_y)
            sends += w_y
        received(forward)
        if stage < 3:
            both_heads(stage, other)
    received(kvv_y)

    shares = []
    for head in range(2):
        mix = attend(3, other, head, True)
        lanes = pl.ds(head * 128, 128)
        values = kvv[:, :, :, head * 128 : head * 128 + 128].reshape(LAT, DV)
        hall[g, :, lanes] = jnp.dot(mix, values, preferred_element_type=F32).astype(BF)
        mine = hall.at[g, :, lanes]
        share = [remote(mine, mine, to) for to in (peer(2), peer(1), peer(-1), sibling)]
        start(share)
        sends += share
        shares.append(share)
    passed = []
    for head in range(2):
        lanes = pl.ds(head * 128, 128)
        for i, dx in ((1, -1), (2, 1), (0, 2)):
            shares[head][i].wait_recv()
            got = hall.at[chip(dx) * 2 + c, :, lanes]
            passed.append(remote(got, got, sibling))
            passed[-1].start()
    sends += passed
    received([shares[0][3], shares[1][3]])
    received(w_y)
    received(passed)

    total = jnp.dot(hall[0], wbuf[0].reshape(256, 256), preferred_element_type=F32)
    for i in range(1, 8):
        total += jnp.dot(hall[i], wbuf[i].reshape(256, 256), preferred_element_type=F32)
    omsg[...] = total.astype(BF).reshape(8, SEL, 256)
    cols = pl.ds(pl.multiple_of(g * 256, 256), 256)
    back = [remote(omsg.at[lax.rem(g + d, 8)], att.at[:, cols], in_group(d)) for d in order]
    start(back)
    sends += back
    att[:, cols] = omsg[g]
    received(back)
    out = pltpu.make_async_copy(att, att_out, lsem.at[2])
    out.start()
    for copy in sends:
        copy.wait_send()
    for copy in to_hbm:
        copy.wait()
    out.wait()


def shards(queries, fresh, cache, selected, position, gain, kv_up, out_weight):
    freqs = np.float32(10000.0) ** (-(np.arange(128) % 32).astype(np.float32) / np.float32(32))
    row = jnp.pad(selected.reshape(1, SEL), ((0, 0), (0, 128 - SEL)))
    vmem = pl.BlockSpec(memory_space=pltpu.VMEM)
    smem = pl.BlockSpec(memory_space=pltpu.SMEM)
    hbm = pl.BlockSpec(memory_space=pl.ANY)
    attended, blended = pl.pallas_call(
        kernel,
        name="blend_attend",
        out_shape=(
            jax.ShapeDtypeStruct((SEL, D), BF),
            jax.ShapeDtypeStruct((KEY, GROUP), BF),
        ),
        in_specs=[vmem] * 4 + [smem] + [vmem] * 4,
        out_specs=(hbm, hbm),
        scratch_shapes=[
            pltpu.VMEM((4, 2, 2, KEY, 256), BF),
            pltpu.VMEM((8, SEL, 384), BF),
            pltpu.VMEM((8, SEL, 384), BF),
            pltpu.VMEM((1, 128), F32),
            pltpu.VMEM((8, 1, 128), F32),
            pltpu.VMEM((8, 4, 16, 256), BF),
            pltpu.VMEM((8, 4, 16, 256), BF),
            pltpu.VMEM((8, 4, 64, 256), BF),
            pltpu.VMEM((1024, LAT), BF),
            pltpu.VMEM((1024, DR), BF),
            pltpu.VMEM((1024, 1), F32),
            pltpu.VMEM((1024, 1), F32),
            pltpu.VMEM((1024, 1), F32),
            pltpu.VMEM((1024, LAT), F32),
            pltpu.VMEM((8, 512, 256), BF),
            pltpu.VMEM((8, SEL, 256), BF),
            pltpu.VMEM((SEL, D), BF),
            pltpu.SemaphoreType.DMA((COPIES,)),
            pltpu.SemaphoreType.DMA((COPIES,)),
            pltpu.SemaphoreType.DMA((3,)),
        ],
        compiler_params=pltpu.CompilerParams(
            collective_id=0, has_side_effects=True, vmem_limit_bytes=56 << 20
        ),
    )(
        queries.reshape(SEL, H * (DN + DR)),
        fresh.reshape(SEL, KEY),
        jnp.swapaxes(cache.reshape(GROUP, KEY), 0, 1),
        row,
        position,
        gain.reshape(1, LAT),
        kv_up,
        out_weight,
        jnp.asarray(freqs.reshape(1, 128)),
    )
    blended = jnp.swapaxes(blended, 0, 1).reshape(1, 1, GROUP, KEY)
    return attended.reshape(1, 1, SEL, D), blended


def solution(mesh):
    return jax.shard_map(
        shards,
        mesh=mesh,
        in_specs=(
            P("prompt", "group", None, None),
            P("prompt", "group", None, None),
            P("prompt", "group", None, None),
            P("prompt", "group", None),
            P("prompt", None),
            P(),
            P("prompt", None),
            P("prompt", None),
        ),
        out_specs=(P("prompt", "group", None, None), P("prompt", "group", None, None)),
        check_vma=False,
    )
```

```python
import functools

import jax
import jax.numpy as jnp
import numpy as np
from jax import lax
from jax.experimental import pallas as pl
from jax.experimental.pallas import tpu as pltpu
from jax.sharding import PartitionSpec as P

D = 2048
H = 16
DN = 128
DR = 64
DV = 128
LAT = 512
KEY = LAT + DR
GROUP = 512
SEL = 64
BF = jnp.bfloat16
F32 = jnp.float32
MESH = pl.DeviceIdType.MESH
EXP_SCALE = float((DN + DR) ** (-0.5) * np.log2(np.e))
COPIES = 96
STAGES = (((0, 0), (0, 1)), ((-1, 0), (1, 1)), ((-1, 1), (1, 0)), ((2, 0), (2, 1)))


def nt(a, b):
    return lax.dot_general(a, b, (((1,), (1,)), ((), ())), preferred_element_type=F32)


def kernel(
    q_ref, fresh_ref, cache_ref, sel_ref, pos_ref, gain_ref, kv_ref, ow_ref, freq_ref,
    att_out, bl_out,
    kbuf, qmsg, qrecv, selmsg, selrecv, kk, kvv, wa, wb, qa, qr, qpl, m_s, l_s, acc, hd, hall, ob, land,
    ssem, rsem, lsem,
):
    g = lax.axis_index("group")
    p = lax.axis_index("prompt")
    x, c = lax.div(g, 2), lax.rem(g, 2)
    z, y = lax.div(p, 4), lax.rem(p, 4)
    other = 1 - c
    used = [0]

    def remote(src, dst, to):
        n = used[0]
        used[0] += 1
        return pltpu.make_async_remote_copy(
            src_ref=src,
            dst_ref=dst,
            send_sem=ssem.at[n],
            recv_sem=rsem.at[n],
            device_id=to,
            device_id_type=MESH,
        )

    def in_group(d):
        return {"group": lax.rem(g + d, 8)}

    def chip(dx):
        return lax.rem(x + dx + 4, 4)

    def peer(dx):
        return {"group": chip(dx) * 2 + c}

    sibling = {"group": x * 2 + other}

    def along_z(d):
        return {"prompt": lax.rem(z + d, 8) * 4 + y}

    def along_y(d):
        return {"prompt": z * 4 + lax.rem(y + d, 4)}

    barrier = pltpu.get_barrier_semaphore()
    everyone = [in_group(d) for d in range(1, 8)]
    everyone += [along_z(d) for d in range(1, 8)] + [along_y(d) for d in range(1, 4)]
    for to in everyone:
        pl.semaphore_signal(barrier, inc=1, device_id=to, device_id_type=MESH)

    part = kv_ref[:, pl.ds(pl.multiple_of(g * 512, 512), 512)]
    kk[z, y] = jnp.concatenate([part[:, :128], part[:, 256:384]], axis=1)
    kvv[z, y] = jnp.concatenate([part[:, 128:256], part[:, 384:]], axis=1)
    wa[z, y] = ow_ref[:, pl.ds(pl.multiple_of(c * 1024, 1024), 512)]
    wb[z, y] = ow_ref[:, pl.ds(pl.multiple_of(c * 1024 + 512, 512), 512)]

    sel_row = sel_ref[...].astype(F32)
    eye = lax.broadcasted_iota(jnp.int32, (SEL, SEL), 0) == lax.broadcasted_iota(
        jnp.int32, (SEL, SEL), 1
    )
    selmsg[...] = jnp.zeros(selmsg.shape, F32)
    selmsg[:, :SEL] = sel_row
    sel_col = jnp.sum(jnp.where(eye, sel_row, 0.0), -1, keepdims=True)
    place = sel_col + (pos_ref[0, g] * GROUP).astype(F32)
    angles = place * freq_ref[...]
    cosine = jnp.cos(angles)
    lane = lax.broadcasted_iota(jnp.int32, (SEL, 128), 1)
    first = lax.rem(lane, 64) < 32
    low = lane < 64
    sine = jnp.sin(angles)
    sine = jnp.where(first, -sine, sine)

    def rotate(v):
        partner = jnp.where(first, pltpu.roll(v, 96, 1), pltpu.roll(v, 32, 1))
        return v * cosine + partner * sine

    for j in range(8):
        t0 = q_ref[:, j * 384 : j * 384 + 128]
        t1 = q_ref[:, j * 384 + 128 : j * 384 + 256].astype(F32)
        t2 = q_ref[:, j * 384 + 256 : j * 384 + 384].astype(F32)
        qmsg[j, :, :128] = t0
        second = jnp.where(low, pltpu.roll(t1, 64, 1), pltpu.roll(t2, 64, 1))
        qmsg[j, :, 128:256] = second.astype(BF)
        qmsg[j, :, 256:] = rotate(jnp.where(low, t1, t2)).astype(BF)

    pl.semaphore_wait(barrier, len(everyone))

    def gather_z(buf):
        return [remote(buf.at[z, y], buf.at[z, y], along_z(d)) for d in range(1, 8)]

    def gather_y(buf):
        return [remote(buf.at[:, y], buf.at[:, y], along_y(d)) for d in range(1, 4)]

    def start(copies):
        for copy in copies:
            copy.start()

    def received(copies):
        for copy in copies:
            copy.wait_recv()

    def ring(buf, lead, k):
        up, down = lax.rem(z - k + 9, 8), lax.rem(z + k - 1, 8)
        if k < 4:
            pair = (buf.at[(up, *lead)], buf.at[(down, *lead)])
        else:
            n = buf.shape[1 + len(lead)] // 2
            pair = (buf.at[(up, *lead, pl.ds(0, n))], buf.at[(down, *lead, pl.ds(n, n))])
        return [remote(pair[0], pair[0], along_z(1)), remote(pair[1], pair[1], along_z(7))]

    kk_z = gather_z(kk)
    start(kk_z)
    sends = list(kk_z)
    wa_y = [remote(wa.at[z, y], wa.at[z, y], along_y(d)) for d in range(1, 4)]
    b_step = ring(wb, (y,), 1)
    order = (4, 3, 5, 2, 6, 1, 7)
    sel_copies = [remote(selmsg, selrecv.at[g], in_group(d)) for d in order]
    start(sel_copies)
    q_copies = [remote(qmsg.at[lax.rem(g + d, 8)], qrecv.at[g], in_group(d)) for d in order]
    start(q_copies)
    kvv_z = gather_z(kvv)
    start(b_step + wa_y + kvv_z)
    sends += sel_copies + q_copies + b_step + wa_y + kvv_z
    qrecv[g] = qmsg[g]
    selrecv[g] = selmsg[...]

    latent = fresh_ref[:, :LAT].astype(F32)
    factor = lax.rsqrt(jnp.mean(latent * latent, -1, keepdims=True) + 1e-06)
    normed = (latent * factor * gain_ref[...].astype(F32).reshape(1, LAT)).astype(BF)
    tail = fresh_ref[:, LAT:].astype(F32)
    turned = rotate(jnp.concatenate([tail, tail], axis=1)).astype(BF)
    columns = lax.broadcasted_iota(jnp.int32, (SEL, GROUP), 1).astype(F32)
    hit = (columns == sel_col).astype(F32)
    taken = jnp.max(hit, 0, keepdims=True) > 0.5
    hit = hit.astype(BF)

    def tn(a, b):
        return lax.dot_general(a, b, (((0,), (0,)), ((), ())), preferred_element_type=F32)

    top = jnp.where(taken, tn(normed, hit), cache_ref[:LAT, :].astype(F32)).astype(BF)
    bottom = jnp.where(taken, tn(turned, hit)[:DR], cache_ref[LAT:, :].astype(F32)).astype(BF)
    for half in range(2):
        cols = slice(half * 256, half * 256 + 256)
        kbuf[0, half, c, :LAT, :] = top[:, cols]
        kbuf[0, half, c, LAT:, :] = bottom[:, cols]

    own = [kbuf.at[0, half, c] for half in range(2)]
    to_sib = [remote(own[i], kbuf.at[0, i, c], sibling) for i in range(2)]
    right = [remote(own[0], kbuf.at[1, 0, c], peer(1)), remote(own[1], kbuf.at[2, 0, c], peer(1))]
    left = [remote(own[1], kbuf.at[1, 1, c], peer(-1)), remote(own[0], kbuf.at[2, 1, c], peer(-1))]
    start([right[0], left[0], to_sib[0], to_sib[1], right[1], left[1]])
    sends += to_sib + right + left
    to_hbm = [
        pltpu.make_async_copy(own[i], bl_out.at[:, pl.ds(i * 256, 256)], lsem.at[i])
        for i in range(2)
    ]
    start(to_hbm)

    m_s[...] = jnp.full(m_s.shape, -1e30, F32)
    l_s[...] = jnp.zeros(l_s.shape, F32)
    acc[...] = jnp.zeros(acc.shape, F32)

    received(kk_z)
    kk_y = gather_y(kk)
    start(kk_y)
    sends += kk_y

    def pass_on(buf, lead, k, step):
        received(step)
        step = ring(buf, lead, k)
        start(step)
        sends.extend(step)
        return step

    b_step = pass_on(wb, (y,), 2, b_step)
    a_step = pass_on(wa, (), 1, wa_y)
    received(kvv_z)
    kvv_y = gather_y(kvv)
    start(kvv_y)
    sends += kvv_y
    received(sel_copies)

    def row_of(src, head):
        at = (src // 2) * 256 + head * 128 + (src % 2) * SEL
        return slice(at, at + SEL)

    for src in range(8):
        column = jnp.sum(jnp.where(eye, selrecv[src][:, :SEL], 0.0), -1, keepdims=True)
        column = column + (pos_ref[0, src] * GROUP).astype(F32)
        for head in range(2):
            qpl[row_of(src, head), :] = column
    b_step = pass_on(wb, (y,), 3, b_step)
    received(q_copies)
    for src in range(8):
        pair = qrecv[src, :, 256:].astype(F32)
        qr[row_of(src, 0), :] = pair[:, :DR].astype(BF)
        qr[row_of(src, 1), :] = pltpu.roll(pair, 64, 1)[:, :DR].astype(BF)
    received(kk_y)
    for head in range(2):
        lanes = slice(head * 128, head * 128 + 128)
        keys = kk[:, :, :, lanes].reshape(LAT, DN)
        plain = qrecv[:, :, lanes].reshape(512, DN)
        qa[:, head] = nt(plain, keys).astype(BF).reshape(4, 128, LAT)
    b_step = pass_on(wb, (y,), 4, b_step)

    def attend(stage, core, at, count, last):
        size = count * 256
        rows = pl.ds(pl.multiple_of(at * 256, 256), size)
        place = qpl[rows, :]
        number = lax.broadcasted_iota(jnp.int32, (size, 256), 1).astype(F32)
        query, turned = qa[pl.ds(at, count)].reshape(size, LAT), qr[rows, :]
        scores = []
        for i, (dx, half) in enumerate(STAGES[stage]):
            base = pos_ref[0, chip(dx) * 2 + core] * GROUP + half * 256
            s = jnp.dot(query, kbuf[stage, i, core, :LAT, :], preferred_element_type=F32)
            s += jnp.dot(turned, kbuf[stage, i, core, LAT:, :], preferred_element_type=F32)
            scores.append(jnp.where(number <= place - base.astype(F32), s, -1e30))
        peak = jnp.maximum(jnp.max(scores[0], -1, keepdims=True), jnp.max(scores[1], -1, keepdims=True))
        old = m_s[rows, :]
        peak = jnp.maximum(old, peak)
        probs = [jnp.exp2((s - peak) * EXP_SCALE) for s in scores]
        decay = jnp.exp2((old - peak) * EXP_SCALE)
        total = l_s[rows, :] * decay + jnp.sum(probs[0] + probs[1], -1, keepdims=True)
        mixed = acc[rows, :] * decay
        for i in range(2):
            mixed += nt(probs[i].astype(BF), kbuf[stage, i, core, :LAT, :])
        if last:
            return (mixed / total).astype(BF)
        m_s[rows, :] = peak
        l_s[rows, :] = total
        acc[rows, :] = mixed

    def step(stage, core):
        def body(tile, carry):
            attend(stage, core, tile * 2, 2, False)
            return carry

        lax.fori_loop(0, 2, body, 0)

    step(0, c)
    received(to_sib)
    received(b_step)
    wb_y = gather_y(wb)
    start(wb_y)
    sends += wb_y
    a_step = pass_on(wa, (), 2, a_step)
    step(0, other)

    received([right[0], left[0]])
    relay = [
        remote(kbuf.at[1, 0, c], kbuf.at[3, 0, c], peer(1)),
        remote(kbuf.at[1, 1, c], kbuf.at[3, 1, c], peer(-1)),
    ]
    start(relay)
    sends += relay
    for stage in range(1, 4):
        if stage == 2:
            received([right[1], left[1]])
        if stage == 3:
            received(relay)
        forward = [remote(kbuf.at[stage, i, c], kbuf.at[stage, i, c], sibling) for i in range(2)]
        start(forward)
        sends += forward
        step(stage, c)
        if stage < 3:
            a_step = pass_on(wa, (), stage + 2, a_step)
        received(forward)
        if stage < 3:
            step(stage, other)
    received(kvv_y)

    values = [kvv[:, :, :, head * 128 : head * 128 + 128].reshape(LAT, DV) for head in range(2)]
    shares = []
    for i, dx in enumerate((2, 1, -1, 0)):
        mix = attend(3, other, chip(dx), 1, True)
        heads = [
            jnp.dot(mix[head * 128 : head * 128 + 128], values[head], preferred_element_type=F32)
            for head in range(2)
        ]
        heads = jnp.concatenate(heads, axis=1).astype(BF)
        if dx:
            hd[i] = heads
            shares.append(remote(hd.at[i], hall.at[g], peer(dx)))
        else:
            hall[g] = heads
            shares.append(remote(hall.at[g], hall.at[g], sibling))
        shares[-1].start()
    sends += shares
    passed = []
    for i, dx in enumerate((2, 1, -1)):
        shares[i].wait_recv()
        got = hall.at[chip(-dx) * 2 + c]
        passed.append(remote(got, got, sibling))
        passed[-1].start()
    sends += passed
    received(a_step + wb_y)
    received(shares[3:] + passed)

    outs = []
    back = []
    for n, weight in enumerate((wa, wb)):
        total = jnp.dot(hall[0], weight[0].reshape(256, 512), preferred_element_type=F32)
        for i in range(1, 8):
            total += jnp.dot(hall[i], weight[i].reshape(256, 512), preferred_element_type=F32)
        ob[n] = total.astype(BF).reshape(2, SEL, 512)
        back.append(remote(ob.at[n, other], land.at[n], sibling))
        back[-1].start()
        cols = pl.ds(pl.multiple_of(c * 1024 + n * 512, 512), 512)
        outs.append(pltpu.make_async_copy(ob.at[n, c], att_out.at[:, cols], lsem.at[2 + n]))
        outs[-1].start()
    sends += back
    for n in range(2):
        back[n].wait_recv()
        cols = pl.ds(pl.multiple_of(other * 1024 + n * 512, 512), 512)
        outs.append(pltpu.make_async_copy(land.at[n], att_out.at[:, cols], lsem.at[4 + n]))
        outs[-1].start()
    for copy in sends:
        copy.wait_send()
    for copy in to_hbm + outs:
        copy.wait()


def shards(queries, fresh, cache, selected, position, gain, kv_up, out_weight):
    freqs = np.float32(10000.0) ** (-(np.arange(128) % 32).astype(np.float32) / np.float32(32))
    vmem = pl.BlockSpec(memory_space=pltpu.VMEM)
    smem = pl.BlockSpec(memory_space=pltpu.SMEM)
    hbm = pl.BlockSpec(memory_space=pl.ANY)
    attended, blended = pl.pallas_call(
        kernel,
        name="blend_attend",
        out_shape=(
            jax.ShapeDtypeStruct((SEL, D), BF),
            jax.ShapeDtypeStruct((KEY, GROUP), BF),
        ),
        in_specs=[vmem] * 4 + [smem] + [vmem] * 4,
        out_specs=(hbm, hbm),
        scratch_shapes=[
            pltpu.VMEM((4, 2, 2, KEY, 256), BF),
            pltpu.VMEM((8, SEL, 384), BF),
            pltpu.VMEM((8, SEL, 384), BF),
            pltpu.VMEM((1, 128), F32),
            pltpu.VMEM((8, 1, 128), F32),
            pltpu.VMEM((8, 4, 16, 256), BF),
            pltpu.VMEM((8, 4, 16, 256), BF),
            pltpu.VMEM((8, 4, 64, 512), BF),
            pltpu.VMEM((8, 4, 64, 512), BF),
            pltpu.VMEM((4, 2, 128, LAT), BF),
            pltpu.VMEM((1024, DR), BF),
            pltpu.VMEM((1024, 1), F32),
            pltpu.VMEM((1024, 1), F32),
            pltpu.VMEM((1024, 1), F32),
            pltpu.VMEM((1024, LAT), F32),
            pltpu.VMEM((3, 128, 256), BF),
            pltpu.VMEM((8, 128, 256), BF),
            pltpu.VMEM((2, 2, SEL, 512), BF),
            pltpu.VMEM((2, SEL, 512), BF),
            pltpu.SemaphoreType.DMA((COPIES,)),
            pltpu.SemaphoreType.DMA((COPIES,)),
            pltpu.SemaphoreType.DMA((6,)),
        ],
        compiler_params=pltpu.CompilerParams(
            collective_id=0, has_side_effects=True, vmem_limit_bytes=56 << 20
        ),
    )(
        queries.reshape(SEL, H * (DN + DR)),
        fresh.reshape(SEL, KEY),
        jnp.swapaxes(cache.reshape(GROUP, KEY), 0, 1),
        selected.reshape(1, SEL),
        position,
        gain,
        kv_up,
        out_weight,
        jnp.asarray(freqs.reshape(1, 128)),
    )
    blended = jnp.swapaxes(blended, 0, 1).reshape(1, 1, GROUP, KEY)
    return attended.reshape(1, 1, SEL, D), blended


def solution(mesh):
    return jax.shard_map(
        shards,
        mesh=mesh,
        in_specs=(
            P("prompt", "group", None, None),
            P("prompt", "group", None, None),
            P("prompt", "group", None, None),
            P("prompt", "group", None),
            P("prompt", None),
            P(),
            P("prompt", None),
            P("prompt", None),
        ),
        out_specs=(P("prompt", "group", None, None), P("prompt", "group", None, None)),
        check_vma=False,
    )
```

```python
import functools

import jax
import jax.numpy as jnp
import numpy as np
from jax import lax
from jax.experimental import pallas as pl
from jax.experimental.pallas import tpu as pltpu
from jax.sharding import PartitionSpec as P

D = 2048
H = 16
DN = 128
DR = 64
DV = 128
LAT = 512
KEY = LAT + DR
GROUP = 512
SEL = 64
BF = jnp.bfloat16
F32 = jnp.float32
MESH = pl.DeviceIdType.MESH
EXP_SCALE = float((DN + DR) ** (-0.5) * np.log2(np.e))
COPIES = 96
STAGES = (((0, 0), (0, 1)), ((-1, 0), (1, 1)), ((-1, 1), (1, 0)), ((2, 0), (2, 1)))


def nt(a, b):
    return lax.dot_general(a, b, (((1,), (1,)), ((), ())), preferred_element_type=F32)


def kernel(
    q_hbm, fresh_hbm, cache_hbm, sel_hbm, pos_hbm, gain_hbm, kv_hbm, ow_hbm, freq_hbm,
    att_out, bl_out,
    q_ref, fresh_ref, cache_ref, sel_ref, pos_ref, gain_ref, kv_ref, freq_ref,
    kbuf, qmsg, qrecv, selmsg, selrecv, kk, kvv, wa, wb, qa, qr, qpl, m_s, l_s, acc, hd, hall, ob, land,
    ssem, rsem, lsem,
):
    g = lax.axis_index("group")
    p = lax.axis_index("prompt")
    x, c = lax.div(g, 2), lax.rem(g, 2)
    z, y = lax.div(p, 4), lax.rem(p, 4)
    other = 1 - c
    used = [0]

    def remote(src, dst, to):
        n = used[0]
        used[0] += 1
        return pltpu.make_async_remote_copy(
            src_ref=src,
            dst_ref=dst,
            send_sem=ssem.at[n],
            recv_sem=rsem.at[n],
            device_id=to,
            device_id_type=MESH,
        )

    def in_group(d):
        return {"group": lax.rem(g + d, 8)}

    def chip(dx):
        return lax.rem(x + dx + 4, 4)

    def peer(dx):
        return {"group": chip(dx) * 2 + c}

    sibling = {"group": x * 2 + other}

    def along_z(d):
        return {"prompt": lax.rem(z + d, 8) * 4 + y}

    def along_y(d):
        return {"prompt": z * 4 + lax.rem(y + d, 4)}

    barrier = pltpu.get_barrier_semaphore()
    everyone = [in_group(d) for d in range(1, 8)]
    everyone += [along_z(d) for d in range(1, 8)] + [along_y(d) for d in range(1, 4)]
    for to in everyone:
        pl.semaphore_signal(barrier, inc=1, device_id=to, device_id_type=MESH)

    fetches = []

    def fetch(src, dst):
        fetches.append(pltpu.make_async_copy(src, dst, lsem.at[8 + len(fetches)]))
        fetches[-1].start()
        return fetches[-1]

    first_needed = [
        fetch(kv_hbm.at[:, pl.ds(pl.multiple_of(g * 512, 512), 512)], kv_ref),
        fetch(sel_hbm, sel_ref),
        fetch(pos_hbm, pos_ref),
        fetch(freq_hbm, freq_ref),
        fetch(q_hbm, q_ref),
        fetch(ow_hbm.at[:, pl.ds(pl.multiple_of(c * 1024, 1024), 512)], wa.at[z, y]),
        fetch(ow_hbm.at[:, pl.ds(pl.multiple_of(c * 1024 + 512, 512), 512)], wb.at[z, y]),
    ]
    later = [fetch(fresh_hbm, fresh_ref), fetch(gain_hbm, gain_ref), fetch(cache_hbm, cache_ref)]
    for copy in first_needed:
        copy.wait()

    part = kv_ref[...]
    kk[z, y] = jnp.concatenate([part[:, :128], part[:, 256:384]], axis=1)
    kvv[z, y] = jnp.concatenate([part[:, 128:256], part[:, 384:]], axis=1)

    sel_row = sel_ref[...].astype(F32)
    eye = lax.broadcasted_iota(jnp.int32, (SEL, SEL), 0) == lax.broadcasted_iota(
        jnp.int32, (SEL, SEL), 1
    )
    selmsg[...] = jnp.zeros(selmsg.shape, F32)
    selmsg[:, :SEL] = sel_row
    sel_col = jnp.sum(jnp.where(eye, sel_row, 0.0), -1, keepdims=True)
    place = sel_col + (pos_ref[0, g] * GROUP).astype(F32)
    angles = place * freq_ref[...]
    cosine = jnp.cos(angles)
    lane = lax.broadcasted_iota(jnp.int32, (SEL, 128), 1)
    first = lax.rem(lane, 64) < 32
    low = lane < 64
    sine = jnp.sin(angles)
    sine = jnp.where(first, -sine, sine)

    def rotate(v):
        partner = jnp.where(first, pltpu.roll(v, 96, 1), pltpu.roll(v, 32, 1))
        return v * cosine + partner * sine

    for j in range(8):
        t0 = q_ref[:, j * 384 : j * 384 + 128]
        t1 = q_ref[:, j * 384 + 128 : j * 384 + 256].astype(F32)
        t2 = q_ref[:, j * 384 + 256 : j * 384 + 384].astype(F32)
        qmsg[j, :, :128] = t0
        second = jnp.where(low, pltpu.roll(t1, 64, 1), pltpu.roll(t2, 64, 1))
        qmsg[j, :, 128:256] = second.astype(BF)
        qmsg[j, :, 256:] = rotate(jnp.where(low, t1, t2)).astype(BF)

    pl.semaphore_wait(barrier, len(everyone))

    def gather_z(buf):
        return [remote(buf.at[z, y], buf.at[z, y], along_z(d)) for d in range(1, 8)]

    def gather_y(buf):
        return [remote(buf.at[:, y], buf.at[:, y], along_y(d)) for d in range(1, 4)]

    def start(copies):
        for copy in copies:
            copy.start()

    def received(copies):
        for copy in copies:
            copy.wait_recv()

    def ring(buf, lead, k):
        up, down = lax.rem(z - k + 9, 8), lax.rem(z + k - 1, 8)
        if k < 4:
            pair = (buf.at[(up, *lead)], buf.at[(down, *lead)])
        else:
            n = buf.shape[1 + len(lead)] // 2
            pair = (buf.at[(up, *lead, pl.ds(0, n))], buf.at[(down, *lead, pl.ds(n, n))])
        return [remote(pair[0], pair[0], along_z(1)), remote(pair[1], pair[1], along_z(7))]

    kk_z = gather_z(kk)
    start(kk_z)
    sends = list(kk_z)
    wa_y = [remote(wa.at[z, y], wa.at[z, y], along_y(d)) for d in range(1, 4)]
    b_step = ring(wb, (y,), 1)
    order = (4, 3, 5, 2, 6, 1, 7)
    sel_copies = [remote(selmsg, selrecv.at[g], in_group(d)) for d in order]
    start(sel_copies)
    q_copies = [remote(qmsg.at[lax.rem(g + d, 8)], qrecv.at[g], in_group(d)) for d in order]
    start(q_copies)
    kvv_z = gather_z(kvv)
    start(b_step + wa_y + kvv_z)
    sends += sel_copies + q_copies + b_step + wa_y + kvv_z
    qrecv[g] = qmsg[g]
    selrecv[g] = selmsg[...]

    for copy in later:
        copy.wait()
    latent = fresh_ref[:, :LAT].astype(F32)
    factor = lax.rsqrt(jnp.mean(latent * latent, -1, keepdims=True) + 1e-06)
    normed = (latent * factor * gain_ref[...].astype(F32).reshape(1, LAT)).astype(BF)
    tail = fresh_ref[:, LAT:].astype(F32)
    turned = rotate(jnp.concatenate([tail, tail], axis=1)).astype(BF)
    columns = lax.broadcasted_iota(jnp.int32, (SEL, GROUP), 1).astype(F32)
    hit = (columns == sel_col).astype(F32)
    taken = jnp.max(hit, 0, keepdims=True) > 0.5
    hit = hit.astype(BF)

    def tn(a, b):
        return lax.dot_general(a, b, (((0,), (0,)), ((), ())), preferred_element_type=F32)

    top = jnp.where(taken, tn(normed, hit), cache_ref[:LAT, :].astype(F32)).astype(BF)
    bottom = jnp.where(taken, tn(turned, hit)[:DR], cache_ref[LAT:, :].astype(F32)).astype(BF)
    for half in range(2):
        cols = slice(half * 256, half * 256 + 256)
        kbuf[0, half, c, :LAT, :] = top[:, cols]
        kbuf[0, half, c, LAT:, :] = bottom[:, cols]

    own = [kbuf.at[0, half, c] for half in range(2)]
    to_sib = [remote(own[i], kbuf.at[0, i, c], sibling) for i in range(2)]
    right = [remote(own[0], kbuf.at[1, 0, c], peer(1)), remote(own[1], kbuf.at[2, 0, c], peer(1))]
    left = [remote(own[1], kbuf.at[1, 1, c], peer(-1)), remote(own[0], kbuf.at[2, 1, c], peer(-1))]
    start([right[0], left[0], to_sib[0], to_sib[1], right[1], left[1]])
    sends += to_sib + right + left
    to_hbm = [
        pltpu.make_async_copy(own[i], bl_out.at[:, pl.ds(i * 256, 256)], lsem.at[i])
        for i in range(2)
    ]
    start(to_hbm)

    m_s[...] = jnp.full(m_s.shape, -1e30, F32)
    l_s[...] = jnp.zeros(l_s.shape, F32)
    acc[...] = jnp.zeros(acc.shape, F32)

    received(kk_z)
    kk_y = gather_y(kk)
    start(kk_y)
    sends += kk_y

    def pass_on(buf, lead, k, step):
        received(step)
        step = ring(buf, lead, k)
        start(step)
        sends.extend(step)
        return step

    b_step = pass_on(wb, (y,), 2, b_step)
    a_step = pass_on(wa, (), 1, wa_y)
    received(kvv_z)
    kvv_y = gather_y(kvv)
    start(kvv_y)
    sends += kvv_y
    received(sel_copies)

    def row_of(src, head):
        at = (src // 2) * 256 + head * 128 + (src % 2) * SEL
        return slice(at, at + SEL)

    for src in range(8):
        column = jnp.sum(jnp.where(eye, selrecv[src][:, :SEL], 0.0), -1, keepdims=True)
        column = column + (pos_ref[0, src] * GROUP).astype(F32)
        for head in range(2):
            qpl[row_of(src, head), :] = column
    b_step = pass_on(wb, (y,), 3, b_step)
    received(q_copies)
    for src in range(8):
        pair = qrecv[src, :, 256:].astype(F32)
        qr[row_of(src, 0), :] = pair[:, :DR].astype(BF)
        qr[row_of(src, 1), :] = pltpu.roll(pair, 64, 1)[:, :DR].astype(BF)
    received(kk_y)
    for head in range(2):
        lanes = slice(head * 128, head * 128 + 128)
        keys = kk[:, :, :, lanes].reshape(LAT, DN)
        plain = qrecv[:, :, lanes].reshape(512, DN)
        qa[:, head] = nt(plain, keys).astype(BF).reshape(4, 128, LAT)
    b_step = pass_on(wb, (y,), 4, b_step)

    def attend(stage, core, at, count, last):
        size = count * 256
        rows = pl.ds(pl.multiple_of(at * 256, 256), size)
        place = qpl[rows, :]
        number = lax.broadcasted_iota(jnp.int32, (size, 256), 1).astype(F32)
        query, turned = qa[pl.ds(at, count)].reshape(size, LAT), qr[rows, :]
        scores = []
        for i, (dx, half) in enumerate(STAGES[stage]):
            base = pos_ref[0, chip(dx) * 2 + core] * GROUP + half * 256
            s = jnp.dot(query, kbuf[stage, i, core, :LAT, :], preferred_element_type=F32)
            s += jnp.dot(turned, kbuf[stage, i, core, LAT:, :], preferred_element_type=F32)
            scores.append(jnp.where(number <= place - base.astype(F32), s, -1e30))
        peak = jnp.maximum(jnp.max(scores[0], -1, keepdims=True), jnp.max(scores[1], -1, keepdims=True))
        old = m_s[rows, :]
        peak = jnp.maximum(old, peak)
        probs = [jnp.exp2((s - peak) * EXP_SCALE) for s in scores]
        decay = jnp.exp2((old - peak) * EXP_SCALE)
        total = l_s[rows, :] * decay + jnp.sum(probs[0] + probs[1], -1, keepdims=True)
        mixed = acc[rows, :] * decay
        for i in range(2):
            mixed += nt(probs[i].astype(BF), kbuf[stage, i, core, :LAT, :])
        if last:
            return (mixed / total).astype(BF)
        m_s[rows, :] = peak
        l_s[rows, :] = total
        acc[rows, :] = mixed

    def step(stage, core):
        def body(tile, carry):
            attend(stage, core, tile * 2, 2, False)
            return carry

        lax.fori_loop(0, 2, body, 0)

    step(0, c)
    received(to_sib)
    received(b_step)
    before, after = lax.rem(y + 3, 4), lax.rem(y + 1, 4)

    def half_y(column, half, to):
        piece = wb.at[pl.ds(half * 4, 4), column]
        return remote(piece, piece, along_y(to))

    wb_y = [half_y(y, 0, 1), half_y(y, 1, 3), half_y(y, 1, 1), half_y(y, 0, 3)]
    start(wb_y)
    sends += wb_y
    a_step = pass_on(wa, (), 2, a_step)
    step(0, other)

    received([right[0], left[0]])
    relay = [
        remote(kbuf.at[1, 0, c], kbuf.at[3, 0, c], peer(1)),
        remote(kbuf.at[1, 1, c], kbuf.at[3, 1, c], peer(-1)),
    ]
    start(relay)
    sends += relay
    for stage in range(1, 4):
        if stage == 2:
            received([right[1], left[1]])
        if stage == 3:
            received(relay)
        forward = [remote(kbuf.at[stage, i, c], kbuf.at[stage, i, c], sibling) for i in range(2)]
        start(forward)
        sends += forward
        step(stage, c)
        if stage < 3:
            a_step = pass_on(wa, (), stage + 2, a_step)
        if stage == 2:
            received(wb_y[:2])
            on_y = [half_y(before, 0, 1), half_y(after, 1, 3)]
            start(on_y)
            sends += on_y
        received(forward)
        if stage < 3:
            step(stage, other)
    received(kvv_y)

    values = [kvv[:, :, :, head * 128 : head * 128 + 128].reshape(LAT, DV) for head in range(2)]
    shares = []
    for i, dx in enumerate((2, 1, -1, 0)):
        mix = attend(3, other, chip(dx), 1, True)
        heads = [
            jnp.dot(mix[head * 128 : head * 128 + 128], values[head], preferred_element_type=F32)
            for head in range(2)
        ]
        heads = jnp.concatenate(heads, axis=1).astype(BF)
        if dx:
            hd[i] = heads
            shares.append(remote(hd.at[i], hall.at[g], peer(dx)))
        else:
            hall[g] = heads
            shares.append(remote(hall.at[g], hall.at[g], sibling))
        shares[-1].start()
    sends += shares
    passed = []
    for i, dx in enumerate((2, 1, -1)):
        shares[i].wait_recv()
        got = hall.at[chip(-dx) * 2 + c]
        passed.append(remote(got, got, sibling))
        passed[-1].start()
    sends += passed
    received(a_step + wb_y[2:] + on_y)
    received(shares[3:] + passed)

    outs = []
    back = []
    for n, weight in enumerate((wa, wb)):
        total = jnp.dot(hall[0], weight[0].reshape(256, 512), preferred_element_type=F32)
        for i in range(1, 8):
            total += jnp.dot(hall[i], weight[i].reshape(256, 512), preferred_element_type=F32)
        ob[n] = total.astype(BF).reshape(2, SEL, 512)
        back.append(remote(ob.at[n, other], land.at[n], sibling))
        back[-1].start()
        cols = pl.ds(pl.multiple_of(c * 1024 + n * 512, 512), 512)
        outs.append(pltpu.make_async_copy(ob.at[n, c], att_out.at[:, cols], lsem.at[2 + n]))
        outs[-1].start()
    sends += back
    for n in range(2):
        back[n].wait_recv()
        cols = pl.ds(pl.multiple_of(other * 1024 + n * 512, 512), 512)
        outs.append(pltpu.make_async_copy(land.at[n], att_out.at[:, cols], lsem.at[4 + n]))
        outs[-1].start()
    for copy in sends:
        copy.wait_send()
    for copy in to_hbm + outs:
        copy.wait()


def shards(queries, fresh, cache, selected, position, gain, kv_up, out_weight):
    freqs = np.float32(10000.0) ** (-(np.arange(128) % 32).astype(np.float32) / np.float32(32))
    hbm = pl.BlockSpec(memory_space=pltpu.HBM)
    anywhere = pl.BlockSpec(memory_space=pl.ANY)
    attended, blended = pl.pallas_call(
        kernel,
        name="blend_attend",
        out_shape=(
            jax.ShapeDtypeStruct((SEL, D), BF),
            jax.ShapeDtypeStruct((KEY, GROUP), BF),
        ),
        in_specs=[hbm] * 9,
        out_specs=(anywhere, anywhere),
        scratch_shapes=[
            pltpu.VMEM((SEL, H * (DN + DR)), BF),
            pltpu.VMEM((SEL, KEY), BF),
            pltpu.VMEM((KEY, GROUP), BF),
            pltpu.VMEM((1, SEL), jnp.int32),
            pltpu.SMEM((1, 8), jnp.int32),
            pltpu.VMEM((LAT,), BF),
            pltpu.VMEM((16, 512), BF),
            pltpu.VMEM((1, 128), F32),
            pltpu.VMEM((4, 2, 2, KEY, 256), BF),
            pltpu.VMEM((8, SEL, 384), BF),
            pltpu.VMEM((8, SEL, 384), BF),
            pltpu.VMEM((1, 128), F32),
            pltpu.VMEM((8, 1, 128), F32),
            pltpu.VMEM((8, 4, 16, 256), BF),
            pltpu.VMEM((8, 4, 16, 256), BF),
            pltpu.VMEM((8, 4, 64, 512), BF),
            pltpu.VMEM((8, 4, 64, 512), BF),
            pltpu.VMEM((4, 2, 128, LAT), BF),
            pltpu.VMEM((1024, DR), BF),
            pltpu.VMEM((1024, 1), F32),
            pltpu.VMEM((1024, 1), F32),
            pltpu.VMEM((1024, 1), F32),
            pltpu.VMEM((1024, LAT), F32),
            pltpu.VMEM((3, 128, 256), BF),
            pltpu.VMEM((8, 128, 256), BF),
            pltpu.VMEM((2, 2, SEL, 512), BF),
            pltpu.VMEM((2, SEL, 512), BF),
            pltpu.SemaphoreType.DMA((COPIES,)),
            pltpu.SemaphoreType.DMA((COPIES,)),
            pltpu.SemaphoreType.DMA((18,)),
        ],
        compiler_params=pltpu.CompilerParams(
            collective_id=0, has_side_effects=True, vmem_limit_bytes=32 << 20
        ),
    )(
        *[
            pltpu.with_memory_space_constraint(operand, pltpu.HBM)
            for operand in (
                queries.reshape(SEL, H * (DN + DR)),
                fresh.reshape(SEL, KEY),
                jnp.swapaxes(cache.reshape(GROUP, KEY), 0, 1),
                selected.reshape(1, SEL),
                position,
                gain,
                kv_up,
                out_weight,
                jnp.asarray(freqs.reshape(1, 128)),
            )
        ]
    )
    blended = jnp.swapaxes(blended, 0, 1).reshape(1, 1, GROUP, KEY)
    return attended.reshape(1, 1, SEL, D), blended


def solution(mesh):
    return jax.shard_map(
        shards,
        mesh=mesh,
        in_specs=(
            P("prompt", "group", None, None),
            P("prompt", "group", None, None),
            P("prompt", "group", None, None),
            P("prompt", "group", None),
            P("prompt", None),
            P(),
            P("prompt", None),
            P("prompt", None),
        ),
        out_specs=(P("prompt", "group", None, None), P("prompt", "group", None, None)),
        check_vma=False,
    )
```

```python
import functools

import jax
import jax.numpy as jnp
import numpy as np
from jax import lax
from jax.experimental import pallas as pl
from jax.experimental.pallas import tpu as pltpu
from jax.sharding import PartitionSpec as P

D = 2048
H = 16
DN = 128
DR = 64
DV = 128
LAT = 512
KEY = LAT + DR
GROUP = 512
SEL = 64
BF = jnp.bfloat16
F32 = jnp.float32
MESH = pl.DeviceIdType.MESH
EXP_SCALE = float((DN + DR) ** (-0.5) * np.log2(np.e))
COPIES = 96
STAGES = (((0, 0), (0, 1)), ((-1, 0), (1, 1)), ((-1, 1), (1, 0)), ((2, 0), (2, 1)))


def nt(a, b):
    return lax.dot_general(a, b, (((1,), (1,)), ((), ())), preferred_element_type=F32)


def kernel(
    q_hbm, fresh_hbm, cache_hbm, sel_hbm, pos_hbm, gain_hbm, kv_hbm, ow_hbm, freq_hbm,
    att_out, bl_out,
    q_ref, fresh_ref, cache_ref, sel_ref, pos_ref, gain_ref, kv_ref, freq_ref,
    kbuf, qmsg, qrecv, selmsg, selrecv, kk, kvv, wa, wb, qa, qr, qpl, m_s, l_s, acc, hd, hall, ob, land,
    ssem, rsem, lsem,
):
    g = lax.axis_index("group")
    p = lax.axis_index("prompt")
    x, c = lax.div(g, 2), lax.rem(g, 2)
    z, y = lax.div(p, 4), lax.rem(p, 4)
    other = 1 - c
    used = [0]

    def remote(src, dst, to):
        n = used[0]
        used[0] += 1
        return pltpu.make_async_remote_copy(
            src_ref=src,
            dst_ref=dst,
            send_sem=ssem.at[n],
            recv_sem=rsem.at[n],
            device_id=to,
            device_id_type=MESH,
        )

    def in_group(d):
        return {"group": lax.rem(g + d, 8)}

    def chip(dx):
        return lax.rem(x + dx + 4, 4)

    def peer(dx):
        return {"group": chip(dx) * 2 + c}

    sibling = {"group": x * 2 + other}

    def along_z(d):
        return {"prompt": lax.rem(z + d, 8) * 4 + y}

    def along_y(d):
        return {"prompt": z * 4 + lax.rem(y + d, 4)}

    barrier = pltpu.get_barrier_semaphore()
    everyone = [in_group(d) for d in range(1, 8)]
    everyone += [along_z(d) for d in range(1, 8)] + [along_y(d) for d in range(1, 4)]
    for to in everyone:
        pl.semaphore_signal(barrier, inc=1, device_id=to, device_id_type=MESH)

    fetches = []

    def fetch(src, dst):
        fetches.append(pltpu.make_async_copy(src, dst, lsem.at[8 + len(fetches)]))
        fetches[-1].start()
        return fetches[-1]

    first_needed = [
        fetch(kv_hbm.at[:, pl.ds(pl.multiple_of(g * 512, 512), 512)], kv_ref),
        fetch(sel_hbm, sel_ref),
        fetch(pos_hbm, pos_ref),
        fetch(freq_hbm, freq_ref),
        fetch(q_hbm, q_ref),
        fetch(ow_hbm.at[:, pl.ds(pl.multiple_of(c * 1024, 1024), 512)], wa.at[z, y]),
        fetch(ow_hbm.at[:, pl.ds(pl.multiple_of(c * 1024 + 512, 512), 512)], wb.at[z, y]),
    ]
    later = [fetch(fresh_hbm, fresh_ref), fetch(gain_hbm, gain_ref), fetch(cache_hbm, cache_ref)]
    for copy in first_needed:
        copy.wait()

    part = kv_ref[...]
    kk[z, y] = jnp.concatenate([part[:, :128], part[:, 256:384]], axis=1)
    kvv[z, y] = jnp.concatenate([part[:, 128:256], part[:, 384:]], axis=1)

    sel_row = sel_ref[...].astype(F32)
    eye = lax.broadcasted_iota(jnp.int32, (SEL, SEL), 0) == lax.broadcasted_iota(
        jnp.int32, (SEL, SEL), 1
    )
    selmsg[...] = jnp.zeros(selmsg.shape, F32)
    selmsg[:, :SEL] = sel_row
    sel_col = jnp.sum(jnp.where(eye, sel_row, 0.0), -1, keepdims=True)
    place = sel_col + (pos_ref[0, g] * GROUP).astype(F32)
    angles = place * freq_ref[...]
    cosine = jnp.cos(angles)
    lane = lax.broadcasted_iota(jnp.int32, (SEL, 128), 1)
    first = lax.rem(lane, 64) < 32
    low = lane < 64
    sine = jnp.sin(angles)
    sine = jnp.where(first, -sine, sine)

    def rotate(v):
        partner = jnp.where(first, pltpu.roll(v, 96, 1), pltpu.roll(v, 32, 1))
        return v * cosine + partner * sine

    for j in range(8):
        t0 = q_ref[:, j * 384 : j * 384 + 128]
        t1 = q_ref[:, j * 384 + 128 : j * 384 + 256].astype(F32)
        t2 = q_ref[:, j * 384 + 256 : j * 384 + 384].astype(F32)
        qmsg[j, :, :128] = t0
        second = jnp.where(low, pltpu.roll(t1, 64, 1), pltpu.roll(t2, 64, 1))
        qmsg[j, :, 128:256] = second.astype(BF)
        qmsg[j, :, 256:] = rotate(jnp.where(low, t1, t2)).astype(BF)

    pl.semaphore_wait(barrier, len(everyone))

    def gather_z(buf):
        return [remote(buf.at[z, y], buf.at[z, y], along_z(d)) for d in range(1, 8)]

    def gather_y(buf):
        return [remote(buf.at[:, y], buf.at[:, y], along_y(d)) for d in range(1, 4)]

    def start(copies):
        for copy in copies:
            copy.start()

    def received(copies):
        for copy in copies:
            copy.wait_recv()

    def ring(view, k, half=None):
        up, down = lax.rem(z - k + 9, 8), lax.rem(z + k - 1, 8)
        if half is not None:
            pieces = [(view(up, half), 1), (view(down, half), 7)]
            pieces = pieces if k < 4 else pieces[half : half + 1]
        elif k < 4:
            pieces = [(view(up, None), 1), (view(down, None), 7)]
        else:
            pieces = [(view(up, 0), 1), (view(down, 1), 7)]
        return [remote(piece, piece, along_z(d)) for piece, d in pieces]

    def view_a(i, half):
        return wa.at[i, pl.ds(half * 2, 2)]

    def view_b(i, half):
        return wb.at[i, y] if half is None else wb.at[i, y, pl.ds(half * 32, 32)]

    kk_z = gather_z(kk)
    start(kk_z)
    sends = list(kk_z)
    wa_y = [remote(wa.at[z, y], wa.at[z, y], along_y(d)) for d in range(1, 4)]
    b_step = ring(view_b, 1)
    order = (4, 3, 5, 2, 6, 1, 7)
    sel_copies = [remote(selmsg, selrecv.at[g], in_group(d)) for d in order]
    start(sel_copies)
    q_copies = [remote(qmsg.at[lax.rem(g + d, 8)], qrecv.at[g], in_group(d)) for d in order]
    start(q_copies)
    kvv_z = gather_z(kvv)
    start(b_step + wa_y + kvv_z)
    sends += sel_copies + q_copies + b_step + wa_y + kvv_z
    qrecv[g] = qmsg[g]
    selrecv[g] = selmsg[...]

    for copy in later:
        copy.wait()
    latent = fresh_ref[:, :LAT].astype(F32)
    factor = lax.rsqrt(jnp.mean(latent * latent, -1, keepdims=True) + 1e-06)
    normed = (latent * factor * gain_ref[...].astype(F32).reshape(1, LAT)).astype(BF)
    tail = fresh_ref[:, LAT:].astype(F32)
    turned = rotate(jnp.concatenate([tail, tail], axis=1)).astype(BF)
    columns = lax.broadcasted_iota(jnp.int32, (SEL, GROUP), 1).astype(F32)
    hit = (columns == sel_col).astype(F32)
    taken = jnp.max(hit, 0, keepdims=True) > 0.5
    hit = hit.astype(BF)

    def tn(a, b):
        return lax.dot_general(a, b, (((0,), (0,)), ((), ())), preferred_element_type=F32)

    top = jnp.where(taken, tn(normed, hit), cache_ref[:LAT, :].astype(F32)).astype(BF)
    bottom = jnp.where(taken, tn(turned, hit)[:DR], cache_ref[LAT:, :].astype(F32)).astype(BF)
    for half in range(2):
        cols = slice(half * 256, half * 256 + 256)
        kbuf[0, half, c, :LAT, :] = top[:, cols]
        kbuf[0, half, c, LAT:, :] = bottom[:, cols]

    own = [kbuf.at[0, half, c] for half in range(2)]
    to_sib = [remote(own[i], kbuf.at[0, i, c], sibling) for i in range(2)]
    right = [remote(own[0], kbuf.at[1, 0, c], peer(1)), remote(own[1], kbuf.at[2, 0, c], peer(1))]
    left = [remote(own[1], kbuf.at[1, 1, c], peer(-1)), remote(own[0], kbuf.at[2, 1, c], peer(-1))]
    start([right[0], left[0], to_sib[0], to_sib[1], right[1], left[1]])
    sends += to_sib + right + left
    to_hbm = [
        pltpu.make_async_copy(own[i], bl_out.at[:, pl.ds(i * 256, 256)], lsem.at[i])
        for i in range(2)
    ]
    start(to_hbm)

    m_s[...] = jnp.full(m_s.shape, -1e30, F32)
    l_s[...] = jnp.zeros(l_s.shape, F32)
    acc[...] = jnp.zeros(acc.shape, F32)

    received(kk_z)
    kk_y = gather_y(kk)
    start(kk_y)
    sends += kk_y

    def pass_b(k, step):
        received(step)
        step = ring(view_b, k)
        start(step)
        sends.extend(step)
        return step

    a_steps = [None, None]

    def pass_a(k, half):
        received(a_steps[half] or [])
        a_steps[half] = ring(view_a, k, half)
        start(a_steps[half])
        sends.extend(a_steps[half])

    b_step = pass_b(2, b_step)
    received(kvv_z)
    kvv_y = gather_y(kvv)
    start(kvv_y)
    sends += kvv_y
    received(sel_copies)

    def row_of(src, head):
        at = (src // 2) * 256 + head * 128 + (src % 2) * SEL
        return slice(at, at + SEL)

    for src in range(8):
        column = jnp.sum(jnp.where(eye, selrecv[src][:, :SEL], 0.0), -1, keepdims=True)
        column = column + (pos_ref[0, src] * GROUP).astype(F32)
        for head in range(2):
            qpl[row_of(src, head), :] = column
    b_step = pass_b(3, b_step)
    received(q_copies)
    for src in range(8):
        pair = qrecv[src, :, 256:].astype(F32)
        qr[row_of(src, 0), :] = pair[:, :DR].astype(BF)
        qr[row_of(src, 1), :] = pltpu.roll(pair, 64, 1)[:, :DR].astype(BF)
    received(kk_y)
    for head in range(2):
        lanes = slice(head * 128, head * 128 + 128)
        keys = kk[:, :, :, lanes].reshape(LAT, DN)
        plain = qrecv[:, :, lanes].reshape(512, DN)
        qa[:, head] = nt(plain, keys).astype(BF).reshape(4, 128, LAT)
    b_step = pass_b(4, b_step)
    received(wa_y)
    pass_a(1, 0)
    pass_a(1, 1)

    def attend(stage, core, at, count, last):
        size = count * 256
        rows = pl.ds(pl.multiple_of(at * 256, 256), size)
        place = qpl[rows, :]
        number = lax.broadcasted_iota(jnp.int32, (size, 256), 1).astype(F32)
        query, turned = qa[pl.ds(at, count)].reshape(size, LAT), qr[rows, :]
        scores = []
        for i, (dx, half) in enumerate(STAGES[stage]):
            base = pos_ref[0, chip(dx) * 2 + core] * GROUP + half * 256
            s = jnp.dot(query, kbuf[stage, i, core, :LAT, :], preferred_element_type=F32)
            s += jnp.dot(turned, kbuf[stage, i, core, LAT:, :], preferred_element_type=F32)
            scores.append(jnp.where(number <= place - base.astype(F32), s, -1e30))
        peak = jnp.maximum(jnp.max(scores[0], -1, keepdims=True), jnp.max(scores[1], -1, keepdims=True))
        old = m_s[rows, :]
        peak = jnp.maximum(old, peak)
        probs = [jnp.exp2((s - peak) * EXP_SCALE) for s in scores]
        decay = jnp.exp2((old - peak) * EXP_SCALE)
        total = l_s[rows, :] * decay + jnp.sum(probs[0] + probs[1], -1, keepdims=True)
        mixed = acc[rows, :] * decay
        for i in range(2):
            mixed += nt(probs[i].astype(BF), kbuf[stage, i, core, :LAT, :])
        if last:
            return (mixed / total).astype(BF)
        m_s[rows, :] = peak
        l_s[rows, :] = total
        acc[rows, :] = mixed

    def step(stage, core):
        def body(tile, carry):
            attend(stage, core, tile * 2, 2, False)
            return carry

        lax.fori_loop(0, 2, body, 0)

    step(0, c)
    received(to_sib)
    received(b_step)
    before, after = lax.rem(y + 3, 4), lax.rem(y + 1, 4)

    def half_y(column, half, to):
        piece = wb.at[pl.ds(half * 4, 4), column]
        return remote(piece, piece, along_y(to))

    wb_y = [half_y(y, 0, 1), half_y(y, 1, 3), half_y(y, 1, 1), half_y(y, 0, 3)]
    start(wb_y)
    sends += wb_y
    step(0, other)
    pass_a(2, 0)

    received([right[0], left[0]])
    relay = [
        remote(kbuf.at[1, 0, c], kbuf.at[3, 0, c], peer(1)),
        remote(kbuf.at[1, 1, c], kbuf.at[3, 1, c], peer(-1)),
    ]
    start(relay)
    sends += relay
    for stage in range(1, 4):
        if stage == 2:
            received([right[1], left[1]])
        if stage == 3:
            received(relay)
        forward = [remote(kbuf.at[stage, i, c], kbuf.at[stage, i, c], sibling) for i in range(2)]
        start(forward)
        sends += forward
        step(stage, c)
        pass_a(stage + 1, 1)
        received(forward)
        if stage < 3:
            step(stage, other)
            pass_a(stage + 2, 0)
        if stage == 1:
            received(wb_y[:2])
            on_y = [half_y(before, 0, 1), half_y(after, 1, 3)]
            start(on_y)
            sends += on_y
    received(kvv_y)

    values = [kvv[:, :, :, head * 128 : head * 128 + 128].reshape(LAT, DV) for head in range(2)]
    shares = []
    for i, dx in enumerate((2, 1, -1, 0)):
        mix = attend(3, other, chip(dx), 1, True)
        heads = [
            jnp.dot(mix[head * 128 : head * 128 + 128], values[head], preferred_element_type=F32)
            for head in range(2)
        ]
        heads = jnp.concatenate(heads, axis=1).astype(BF)
        if dx:
            hd[i] = heads
            shares.append(remote(hd.at[i], hall.at[g], peer(dx)))
        else:
            hall[g] = heads
            shares.append(remote(hall.at[g], hall.at[g], sibling))
        shares[-1].start()
    sends += shares
    received(a_steps[0] + a_steps[1] + wb_y[2:] + on_y)

    def project(total, source):
        part = [
            jnp.dot(hall[source], weight[source].reshape(256, 512), preferred_element_type=F32)
            for weight in (wa, wb)
        ]
        return part if total is None else [a + b for a, b in zip(total, part)]

    totals = project(None, g)
    passed = []
    for i, dx in ((3, 0), (1, 1), (2, -1), (0, 2)):
        shares[i].wait_recv()
        if dx:
            source = chip(-dx) * 2 + c
            passed.append(remote(hall.at[source], hall.at[source], sibling))
            passed[-1].start()
        else:
            source = x * 2 + other
        totals = project(totals, source)
    sends += passed
    for i, dx in enumerate((1, -1, 2)):
        passed[i].wait_recv()
        totals = project(totals, chip(-dx) * 2 + other)

    outs = []
    back = []
    for n, total in enumerate(totals):
        ob[n] = total.astype(BF).reshape(2, SEL, 512)
        back.append(remote(ob.at[n, other], land.at[n], sibling))
        back[-1].start()
        cols = pl.ds(pl.multiple_of(c * 1024 + n * 512, 512), 512)
        outs.append(pltpu.make_async_copy(ob.at[n, c], att_out.at[:, cols], lsem.at[2 + n]))
        outs[-1].start()
    sends += back
    for n in range(2):
        back[n].wait_recv()
        cols = pl.ds(pl.multiple_of(other * 1024 + n * 512, 512), 512)
        outs.append(pltpu.make_async_copy(land.at[n], att_out.at[:, cols], lsem.at[4 + n]))
        outs[-1].start()
    for copy in sends:
        copy.wait_send()
    for copy in to_hbm + outs:
        copy.wait()


def shards(queries, fresh, cache, selected, position, gain, kv_up, out_weight):
    freqs = np.float32(10000.0) ** (-(np.arange(128) % 32).astype(np.float32) / np.float32(32))
    hbm = pl.BlockSpec(memory_space=pltpu.HBM)
    anywhere = pl.BlockSpec(memory_space=pl.ANY)
    attended, blended = pl.pallas_call(
        kernel,
        name="blend_attend",
        out_shape=(
            jax.ShapeDtypeStruct((SEL, D), BF),
            jax.ShapeDtypeStruct((KEY, GROUP), BF),
        ),
        in_specs=[hbm] * 9,
        out_specs=(anywhere, anywhere),
        scratch_shapes=[
            pltpu.VMEM((SEL, H * (DN + DR)), BF),
            pltpu.VMEM((SEL, KEY), BF),
            pltpu.VMEM((KEY, GROUP), BF),
            pltpu.VMEM((1, SEL), jnp.int32),
            pltpu.SMEM((1, 8), jnp.int32),
            pltpu.VMEM((LAT,), BF),
            pltpu.VMEM((16, 512), BF),
            pltpu.VMEM((1, 128), F32),
            pltpu.VMEM((4, 2, 2, KEY, 256), BF),
            pltpu.VMEM((8, SEL, 384), BF),
            pltpu.VMEM((8, SEL, 384), BF),
            pltpu.VMEM((1, 128), F32),
            pltpu.VMEM((8, 1, 128), F32),
            pltpu.VMEM((8, 4, 16, 256), BF),
            pltpu.VMEM((8, 4, 16, 256), BF),
            pltpu.VMEM((8, 4, 64, 512), BF),
            pltpu.VMEM((8, 4, 64, 512), BF),
            pltpu.VMEM((4, 2, 128, LAT), BF),
            pltpu.VMEM((1024, DR), BF),
            pltpu.VMEM((1024, 1), F32),
            pltpu.VMEM((1024, 1), F32),
            pltpu.VMEM((1024, 1), F32),
            pltpu.VMEM((1024, LAT), F32),
            pltpu.VMEM((3, 128, 256), BF),
            pltpu.VMEM((8, 128, 256), BF),
            pltpu.VMEM((2, 2, SEL, 512), BF),
            pltpu.VMEM((2, SEL, 512), BF),
            pltpu.SemaphoreType.DMA((COPIES,)),
            pltpu.SemaphoreType.DMA((COPIES,)),
            pltpu.SemaphoreType.DMA((18,)),
        ],
        compiler_params=pltpu.CompilerParams(
            collective_id=0, has_side_effects=True, vmem_limit_bytes=32 << 20
        ),
    )(
        *[
            pltpu.with_memory_space_constraint(operand, pltpu.HBM)
            for operand in (
                queries.reshape(SEL, H * (DN + DR)),
                fresh.reshape(SEL, KEY),
                jnp.swapaxes(cache.reshape(GROUP, KEY), 0, 1),
                selected.reshape(1, SEL),
                position,
                gain,
                kv_up,
                out_weight,
                jnp.asarray(freqs.reshape(1, 128)),
            )
        ]
    )
    blended = jnp.swapaxes(blended, 0, 1).reshape(1, 1, GROUP, KEY)
    return attended.reshape(1, 1, SEL, D), blended


def solution(mesh):
    return jax.shard_map(
        shards,
        mesh=mesh,
        in_specs=(
            P("prompt", "group", None, None),
            P("prompt", "group", None, None),
            P("prompt", "group", None, None),
            P("prompt", "group", None),
            P("prompt", None),
            P(),
            P("prompt", None),
            P("prompt", None),
        ),
        out_specs=(P("prompt", "group", None, None), P("prompt", "group", None, None)),
        check_vma=False,
    )
```

```python
import functools

import jax
import jax.numpy as jnp
import numpy as np
from jax import lax
from jax.experimental import pallas as pl
from jax.experimental.pallas import tpu as pltpu
from jax.sharding import PartitionSpec as P

D = 2048
H = 16
DN = 128
DR = 64
DV = 128
LAT = 512
KEY = LAT + DR
GROUP = 512
SEL = 64
BF = jnp.bfloat16
F32 = jnp.float32
MESH = pl.DeviceIdType.MESH
EXP_SCALE = float((DN + DR) ** (-0.5) * np.log2(np.e))
COPIES = 112
STAGES = (((0, 0), (0, 1)), ((-1, 0), (1, 1)), ((-1, 1), (1, 0)), ((2, 0), (2, 1)))


def nt(a, b):
    return lax.dot_general(a, b, (((1,), (1,)), ((), ())), preferred_element_type=F32)


def kernel(
    q_hbm, fresh_hbm, cache_hbm, sel_hbm, pos_hbm, gain_hbm, kv_hbm, ow_hbm, freq_hbm,
    att_out, bl_out,
    q_ref, fresh_ref, cache_ref, sel_ref, pos_ref, gain_ref, kv_ref, freq_ref,
    kbuf, qmsg, qrecv, selmsg, selrecv, kk, kvv, wa, wb, qa, qr, qpl, m_s, l_s, acc, hd, hall, ob, land,
    ssem, rsem, lsem,
):
    g = lax.axis_index("group")
    p = lax.axis_index("prompt")
    x, c = lax.div(g, 2), lax.rem(g, 2)
    z, y = lax.div(p, 4), lax.rem(p, 4)
    other = 1 - c
    used = [0]

    def remote(src, dst, to):
        n = used[0]
        used[0] += 1
        return pltpu.make_async_remote_copy(
            src_ref=src,
            dst_ref=dst,
            send_sem=ssem.at[n],
            recv_sem=rsem.at[n],
            device_id=to,
            device_id_type=MESH,
        )

    def in_group(d):
        return {"group": lax.rem(g + d, 8)}

    def chip(dx):
        return lax.rem(x + dx + 4, 4)

    def peer(dx):
        return {"group": chip(dx) * 2 + c}

    sibling = {"group": x * 2 + other}

    def along_z(d):
        return {"prompt": lax.rem(z + d, 8) * 4 + y}

    def along_y(d):
        return {"prompt": z * 4 + lax.rem(y + d, 4)}

    barrier = pltpu.get_barrier_semaphore()
    everyone = [in_group(d) for d in range(1, 8)]
    everyone += [along_z(d) for d in (1, 7, 2, 6)] + [along_y(d) for d in range(1, 4)]
    for to in everyone:
        pl.semaphore_signal(barrier, inc=1, device_id=to, device_id_type=MESH)

    fetches = []

    def fetch(src, dst):
        fetches.append(pltpu.make_async_copy(src, dst, lsem.at[8 + len(fetches)]))
        fetches[-1].start()
        return fetches[-1]

    first_needed = [
        fetch(kv_hbm.at[:, pl.ds(pl.multiple_of(g * 512, 512), 512)], kv_ref),
        fetch(sel_hbm, sel_ref),
        fetch(pos_hbm, pos_ref),
        fetch(freq_hbm, freq_ref),
        fetch(q_hbm, q_ref),
        fetch(ow_hbm.at[:, pl.ds(pl.multiple_of(c * 1024, 1024), 512)], wa.at[z, y]),
        fetch(ow_hbm.at[:, pl.ds(pl.multiple_of(c * 1024 + 512, 512), 512)], wb.at[z, y]),
    ]
    later = [fetch(fresh_hbm, fresh_ref), fetch(gain_hbm, gain_ref), fetch(cache_hbm, cache_ref)]
    for copy in first_needed:
        copy.wait()

    part = kv_ref[...]
    kk[z, y] = jnp.concatenate([part[:, :128], part[:, 256:384]], axis=1)
    kvv[z, y] = jnp.concatenate([part[:, 128:256], part[:, 384:]], axis=1)

    sel_row = sel_ref[...].astype(F32)
    eye = lax.broadcasted_iota(jnp.int32, (SEL, SEL), 0) == lax.broadcasted_iota(
        jnp.int32, (SEL, SEL), 1
    )
    selmsg[...] = jnp.zeros(selmsg.shape, F32)
    selmsg[:, :SEL] = sel_row
    sel_col = jnp.sum(jnp.where(eye, sel_row, 0.0), -1, keepdims=True)
    place = sel_col + (pos_ref[0, g] * GROUP).astype(F32)
    angles = place * freq_ref[...]
    cosine = jnp.cos(angles)
    lane = lax.broadcasted_iota(jnp.int32, (SEL, 128), 1)
    first = lax.rem(lane, 64) < 32
    low = lane < 64
    sine = jnp.sin(angles)
    sine = jnp.where(first, -sine, sine)

    def rotate(v):
        partner = jnp.where(first, pltpu.roll(v, 96, 1), pltpu.roll(v, 32, 1))
        return v * cosine + partner * sine

    for j in range(8):
        t0 = q_ref[:, j * 384 : j * 384 + 128]
        t1 = q_ref[:, j * 384 + 128 : j * 384 + 256].astype(F32)
        t2 = q_ref[:, j * 384 + 256 : j * 384 + 384].astype(F32)
        qmsg[j, :, :128] = t0
        second = jnp.where(low, pltpu.roll(t1, 64, 1), pltpu.roll(t2, 64, 1))
        qmsg[j, :, 128:256] = second.astype(BF)
        qmsg[j, :, 256:] = rotate(jnp.where(low, t1, t2)).astype(BF)

    pl.semaphore_wait(barrier, len(everyone))

    def near_z(buf):
        return [remote(buf.at[z, y], buf.at[z, y], along_z(d)) for d in (1, 7, 2, 6)]

    def far_z(buf):
        pieces = [(buf.at[lax.rem(z + d, 8), y], to) for d, to in ((7, 2), (1, 6), (6, 2))]
        return [remote(piece, piece, along_z(to)) for piece, to in pieces]

    def gather_y(buf):
        return [remote(buf.at[:, y], buf.at[:, y], along_y(d)) for d in range(1, 4)]

    def start(copies):
        for copy in copies:
            copy.start()

    def received(copies):
        for copy in copies:
            copy.wait_recv()

    def ring(view, k, half=None):
        up, down = lax.rem(z - k + 9, 8), lax.rem(z + k - 1, 8)
        if half is not None:
            pieces = [(view(up, half), 1), (view(down, half), 7)]
            pieces = pieces if k < 4 else pieces[half : half + 1]
        elif k < 4:
            pieces = [(view(up, None), 1), (view(down, None), 7)]
        else:
            pieces = [(view(up, 0), 1), (view(down, 1), 7)]
        return [remote(piece, piece, along_z(d)) for piece, d in pieces]

    def view_a(i, half):
        return wa.at[i, pl.ds(half * 2, 2)]

    def view_b(i, half):
        return wb.at[i, y] if half is None else wb.at[i, y, pl.ds(half * 32, 32)]

    kk_near = near_z(kk)
    start(kk_near)
    sends = list(kk_near)
    wa_y = [remote(wa.at[z, y], wa.at[z, y], along_y(d)) for d in range(1, 4)]
    b_step = ring(view_b, 1)
    order = (4, 3, 5, 2, 6, 1, 7)
    sel_copies = [remote(selmsg, selrecv.at[g], in_group(d)) for d in order]
    start(sel_copies)
    q_copies = [remote(qmsg.at[lax.rem(g + d, 8)], qrecv.at[g], in_group(d)) for d in order]
    start(q_copies)
    start(b_step + wa_y)
    sends += sel_copies + q_copies + b_step + wa_y
    qrecv[g] = qmsg[g]
    selrecv[g] = selmsg[...]

    for copy in later:
        copy.wait()
    latent = fresh_ref[:, :LAT].astype(F32)
    factor = lax.rsqrt(jnp.mean(latent * latent, -1, keepdims=True) + 1e-06)
    normed = (latent * factor * gain_ref[...].astype(F32).reshape(1, LAT)).astype(BF)
    tail = fresh_ref[:, LAT:].astype(F32)
    turned = rotate(jnp.concatenate([tail, tail], axis=1)).astype(BF)
    columns = lax.broadcasted_iota(jnp.int32, (SEL, GROUP), 1).astype(F32)
    hit = (columns == sel_col).astype(F32)
    taken = jnp.max(hit, 0, keepdims=True) > 0.5
    hit = hit.astype(BF)

    def tn(a, b):
        return lax.dot_general(a, b, (((0,), (0,)), ((), ())), preferred_element_type=F32)

    top = jnp.where(taken, tn(normed, hit), cache_ref[:LAT, :].astype(F32)).astype(BF)
    bottom = jnp.where(taken, tn(turned, hit)[:DR], cache_ref[LAT:, :].astype(F32)).astype(BF)
    for half in range(2):
        cols = slice(half * 256, half * 256 + 256)
        kbuf[0, half, c, :LAT, :] = top[:, cols]
        kbuf[0, half, c, LAT:, :] = bottom[:, cols]

    own = [kbuf.at[0, half, c] for half in range(2)]
    to_sib = [remote(own[i], kbuf.at[0, i, c], sibling) for i in range(2)]
    right = [remote(own[0], kbuf.at[1, 0, c], peer(1)), remote(own[1], kbuf.at[2, 0, c], peer(1))]
    left = [remote(own[1], kbuf.at[1, 1, c], peer(-1)), remote(own[0], kbuf.at[2, 1, c], peer(-1))]
    start([right[0], left[0], to_sib[0], to_sib[1], right[1], left[1]])
    sends += to_sib + right + left
    to_hbm = [
        pltpu.make_async_copy(own[i], bl_out.at[:, pl.ds(i * 256, 256)], lsem.at[i])
        for i in range(2)
    ]
    start(to_hbm)

    m_s[...] = jnp.full(m_s.shape, -1e30, F32)
    l_s[...] = jnp.zeros(l_s.shape, F32)
    acc[...] = jnp.zeros(acc.shape, F32)

    received(kk_near)
    kk_far = far_z(kk)
    start(kk_far)
    sends += kk_far

    def pass_b(k, step):
        received(step)
        step = ring(view_b, k)
        start(step)
        sends.extend(step)
        return step

    a_steps = [None, None]

    def pass_a(k, half):
        received(a_steps[half] or [])
        a_steps[half] = ring(view_a, k, half)
        start(a_steps[half])
        sends.extend(a_steps[half])

    b_step = pass_b(2, b_step)
    received(wa_y)
    pass_a(1, 0)
    kvv_near = near_z(kvv)
    start(kvv_near)
    sends += kvv_near
    received(kk_far)
    kk_y = gather_y(kk)
    start(kk_y)
    sends += kk_y

    before, after = lax.rem(y + 3, 4), lax.rem(y + 1, 4)
    y_right, y_left, on_y = {}, {}, []

    def y_piece(column, offset, to):
        piece = wb.at[lax.rem(z + offset, 8), column]
        copy = remote(piece, piece, along_y(to))
        copy.start()
        sends.append(copy)
        return copy

    def send_y(right, left):
        for a, b in zip(right, left):
            y_right[a] = y_piece(y, a, 1)
            y_left[b] = y_piece(y, b, 3)

    def relay_y(right, left):
        for a in right:
            y_right.pop(a).wait_recv()
            on_y.append(y_piece(before, a, 1))
        for b in left:
            y_left.pop(b).wait_recv()
            on_y.append(y_piece(after, b, 3))

    send_y((0, 1, 7), (0, 7, 1))
    received(sel_copies)

    def row_of(src, head):
        at = (src // 2) * 256 + head * 128 + (src % 2) * SEL
        return slice(at, at + SEL)

    for src in range(8):
        column = jnp.sum(jnp.where(eye, selrecv[src][:, :SEL], 0.0), -1, keepdims=True)
        column = column + (pos_ref[0, src] * GROUP).astype(F32)
        for head in range(2):
            qpl[row_of(src, head), :] = column
    b_step = pass_b(3, b_step)
    send_y((2, 6), (6, 2))
    pass_a(1, 1)
    received(q_copies)
    for src in range(8):
        pair = qrecv[src, :, 256:].astype(F32)
        qr[row_of(src, 0), :] = pair[:, :DR].astype(BF)
        qr[row_of(src, 1), :] = pltpu.roll(pair, 64, 1)[:, :DR].astype(BF)
    received(kk_y)
    for head in range(2):
        lanes = slice(head * 128, head * 128 + 128)
        keys = kk[:, :, :, lanes].reshape(LAT, DN)
        plain = qrecv[:, :, lanes].reshape(512, DN)
        qa[:, head] = nt(plain, keys).astype(BF).reshape(4, 128, LAT)
    b_step = pass_b(4, b_step)
    send_y((3, 5), (5, 3))
    received(kvv_near)
    kvv_far = far_z(kvv)
    start(kvv_far)
    sends += kvv_far
    pass_a(2, 0)

    def tile(at):
        return pl.ds(at * 256 if isinstance(at, int) else pl.multiple_of(at * 256, 256), 256)

    def score(stage, core, at):
        rows = tile(at)
        place = qpl[rows, :]
        number = lax.broadcasted_iota(jnp.int32, (256, 256), 1).astype(F32)
        query, turned = qa[at].reshape(256, LAT), qr[rows, :]
        scores = []
        for i, (dx, half) in enumerate(STAGES[stage]):
            base = pos_ref[0, chip(dx) * 2 + core] * GROUP + half * 256
            s = jnp.dot(query, kbuf[stage, i, core, :LAT, :], preferred_element_type=F32)
            s += jnp.dot(turned, kbuf[stage, i, core, LAT:, :], preferred_element_type=F32)
            scores.append(jnp.where(number <= place - base.astype(F32), s, -1e30))
        return scores

    def mix(stage, core, at, scores, last):
        rows = tile(at)
        old = m_s[rows, :]
        peak = jnp.max(jnp.maximum(scores[0], scores[1]), -1, keepdims=True)
        peak = jnp.maximum(old, peak)
        probs = [jnp.exp2((s - peak) * EXP_SCALE) for s in scores]
        decay = jnp.exp2((old - peak) * EXP_SCALE)
        total = l_s[rows, :] * decay + jnp.sum(probs[0] + probs[1], -1, keepdims=True)
        mixed = acc[rows, :] * decay
        for i in range(2):
            mixed += nt(probs[i].astype(BF), kbuf[stage, i, core, :LAT, :])
        if last:
            return (mixed / total).astype(BF)
        m_s[rows, :] = peak
        l_s[rows, :] = total
        acc[rows, :] = mixed

    def step(stage, core):
        scores = score(stage, core, 0)
        for at in range(4):
            ahead = score(stage, core, at + 1) if at < 3 else None
            mix(stage, core, at, scores, False)
            scores = ahead

    step(0, c)
    received(to_sib)
    pass_a(2, 1)
    received(kvv_far)
    kvv_y = gather_y(kvv)
    start(kvv_y)
    sends += kvv_y
    relay_y((0, 1), (7,))
    step(0, other)
    received(b_step)
    send_y((4,), (4,))

    received([right[0], left[0]])
    relay = [
        remote(kbuf.at[1, 0, c], kbuf.at[3, 0, c], peer(1)),
        remote(kbuf.at[1, 1, c], kbuf.at[3, 1, c], peer(-1)),
    ]
    start(relay)
    sends += relay
    for stage in range(1, 4):
        if stage == 2:
            received([right[1], left[1]])
        if stage == 3:
            received(relay)
        forward = [remote(kbuf.at[stage, i, c], kbuf.at[stage, i, c], sibling) for i in range(2)]
        start(forward)
        sends += forward
        step(stage, c)
        if stage < 3:
            pass_a(stage + 2, 0)
            relay_y(*((((2,), (6,)), ((), (4,)))[stage - 1]))
        received(forward)
        if stage < 3:
            step(stage, other)
            pass_a(stage + 2, 1)
        if stage == 1:
            relay_y((3,), (5,))
    received(kvv_y)

    values = [kvv[:, :, :, head * 128 : head * 128 + 128].reshape(LAT, DV) for head in range(2)]
    shares = []
    targets = (2, 1, -1, 0)
    scores = score(3, other, chip(2))
    for i, dx in enumerate(targets):
        ahead = score(3, other, chip(targets[i + 1])) if i < 3 else None
        mixed = mix(3, other, chip(dx), scores, True)
        scores = ahead
        heads = [
            jnp.dot(mixed[head * 128 : head * 128 + 128], values[head], preferred_element_type=F32)
            for head in range(2)
        ]
        heads = jnp.concatenate(heads, axis=1).astype(BF)
        if dx:
            hd[i] = heads
            shares.append(remote(hd.at[i], hall.at[g], peer(dx)))
        else:
            hall[g] = heads
            shares.append(remote(hall.at[g], hall.at[g], sibling))
        shares[-1].start()
    sends += shares
    received(a_steps[0] + a_steps[1] + list(y_right.values()) + list(y_left.values()) + on_y)

    def project(total, source):
        part = [
            jnp.dot(hall[source], weight[source].reshape(256, 512), preferred_element_type=F32)
            for weight in (wa, wb)
        ]
        return part if total is None else [a + b for a, b in zip(total, part)]

    totals = project(None, g)
    passed = []
    for i, dx in ((3, 0), (1, 1), (2, -1), (0, 2)):
        shares[i].wait_recv()
        if dx:
            source = chip(-dx) * 2 + c
            passed.append(remote(hall.at[source], hall.at[source], sibling))
            passed[-1].start()
        else:
            source = x * 2 + other
        totals = project(totals, source)
    sends += passed
    for i, dx in enumerate((1, -1, 2)):
        passed[i].wait_recv()
        totals = project(totals, chip(-dx) * 2 + other)

    outs = []
    back = []
    for n, total in enumerate(totals):
        ob[n] = total.astype(BF).reshape(2, SEL, 512)
        back.append(remote(ob.at[n, other], land.at[n], sibling))
        back[-1].start()
        cols = pl.ds(pl.multiple_of(c * 1024 + n * 512, 512), 512)
        outs.append(pltpu.make_async_copy(ob.at[n, c], att_out.at[:, cols], lsem.at[2 + n]))
        outs[-1].start()
    sends += back
    for n in range(2):
        back[n].wait_recv()
        cols = pl.ds(pl.multiple_of(other * 1024 + n * 512, 512), 512)
        outs.append(pltpu.make_async_copy(land.at[n], att_out.at[:, cols], lsem.at[4 + n]))
        outs[-1].start()
    for copy in sends:
        copy.wait_send()
    for copy in to_hbm + outs:
        copy.wait()


def shards(queries, fresh, cache, selected, position, gain, kv_up, out_weight):
    freqs = np.float32(10000.0) ** (-(np.arange(128) % 32).astype(np.float32) / np.float32(32))
    hbm = pl.BlockSpec(memory_space=pltpu.HBM)
    anywhere = pl.BlockSpec(memory_space=pl.ANY)
    attended, blended = pl.pallas_call(
        kernel,
        name="blend_attend",
        out_shape=(
            jax.ShapeDtypeStruct((SEL, D), BF),
            jax.ShapeDtypeStruct((KEY, GROUP), BF),
        ),
        in_specs=[hbm] * 9,
        out_specs=(anywhere, anywhere),
        scratch_shapes=[
            pltpu.VMEM((SEL, H * (DN + DR)), BF),
            pltpu.VMEM((SEL, KEY), BF),
            pltpu.VMEM((KEY, GROUP), BF),
            pltpu.VMEM((1, SEL), jnp.int32),
            pltpu.SMEM((1, 8), jnp.int32),
            pltpu.VMEM((LAT,), BF),
            pltpu.VMEM((16, 512), BF),
            pltpu.VMEM((1, 128), F32),
            pltpu.VMEM((4, 2, 2, KEY, 256), BF),
            pltpu.VMEM((8, SEL, 384), BF),
            pltpu.VMEM((8, SEL, 384), BF),
            pltpu.VMEM((1, 128), F32),
            pltpu.VMEM((8, 1, 128), F32),
            pltpu.VMEM((8, 4, 16, 256), BF),
            pltpu.VMEM((8, 4, 16, 256), BF),
            pltpu.VMEM((8, 4, 64, 512), BF),
            pltpu.VMEM((8, 4, 64, 512), BF),
            pltpu.VMEM((4, 2, 128, LAT), BF),
            pltpu.VMEM((1024, DR), BF),
            pltpu.VMEM((1024, 1), F32),
            pltpu.VMEM((1024, 1), F32),
            pltpu.VMEM((1024, 1), F32),
            pltpu.VMEM((1024, LAT), F32),
            pltpu.VMEM((3, 128, 256), BF),
            pltpu.VMEM((8, 128, 256), BF),
            pltpu.VMEM((2, 2, SEL, 512), BF),
            pltpu.VMEM((2, SEL, 512), BF),
            pltpu.SemaphoreType.DMA((COPIES,)),
            pltpu.SemaphoreType.DMA((COPIES,)),
            pltpu.SemaphoreType.DMA((18,)),
        ],
        compiler_params=pltpu.CompilerParams(
            collective_id=0, has_side_effects=True, vmem_limit_bytes=32 << 20
        ),
    )(
        *[
            pltpu.with_memory_space_constraint(operand, pltpu.HBM)
            for operand in (
                queries.reshape(SEL, H * (DN + DR)),
                fresh.reshape(SEL, KEY),
                jnp.swapaxes(cache.reshape(GROUP, KEY), 0, 1),
                selected.reshape(1, SEL),
                position,
                gain,
                kv_up,
                out_weight,
                jnp.asarray(freqs.reshape(1, 128)),
            )
        ]
    )
    blended = jnp.swapaxes(blended, 0, 1).reshape(1, 1, GROUP, KEY)
    return attended.reshape(1, 1, SEL, D), blended


def solution(mesh):
    return jax.shard_map(
        shards,
        mesh=mesh,
        in_specs=(
            P("prompt", "group", None, None),
            P("prompt", "group", None, None),
            P("prompt", "group", None, None),
            P("prompt", "group", None),
            P("prompt", None),
            P(),
            P("prompt", None),
            P("prompt", None),
        ),
        out_specs=(P("prompt", "group", None, None), P("prompt", "group", None, None)),
        check_vma=False,
    )
```
